512 devices in a mesh: prow: 16 (over z), pcol: 32 (over x, y, core).
Axes of the slice: x: 4, y: 4, z: 16, core: 2. Of those that a mesh axis runs over, the one named last changes fastest.
Arguments:
- matrix: bfloat16 [3, 8192, 1, 16384], P(None, 'prow', None, 'pcol'), may hold values from -6 to 6
- pattern: int32 [48, 32], replicated, may hold values 0 or 1
- inverses: bfloat16 [2, 512, 512], replicated, may hold values from -0.01171875 to 0.01171875
- pivots: int32 [2, 3], replicated, may hold values from 0 to 47, as said below
Outputs:
- factored: bfloat16 [3, 8192, 1, 16384], P(None, 'prow', None, 'pcol')
The draws below stay inside these ranges and needn't reach their ends.
Inputs may be any that keep to these rules, and one draw needn't show every extreme that they name: pivots[s] = (a, b, c) with a and b block rows in 0 .. 47 and c a block column in 0 .. 31; the 4 numbers a and b over all steps are all different, and so are the 2 numbers c; b mod 16 = (a + 8) mod 16 for every step; block row 0 and block row 47 are among the b, and block column 31 is among the c.
All inputs are finite; a program needn't handle non-finite values.
Results may differ from the reference program's by a relative error of at most 0.0068.
Values may be sent and summed in bfloat16 or wider, within the bound.
A program may use at most 64 MiB of HBM per device.

```python
import jax
import jax.numpy as jnp
from jax import lax

NB = 512
RB_DEV = 3
CB_DEV = 1
STEPS = 2
MB = 48
NC = 32
N_PROW = 16
N_PCOL = 32


def draw_pivots(key, part):
    half_axis = N_PROW // 2
    step_ids = jnp.arange(STEPS, dtype=jnp.int32)
    owner_second = jnp.where(step_ids == 0, 0, jnp.where(step_ids == STEPS - 1, N_PROW - 1, step_ids)).astype(jnp.int32)
    owner_first = ((owner_second + half_axis) % N_PROW).astype(jnp.int32)
    slots_first = jax.random.randint(jax.random.fold_in(key, 11), (STEPS,), 0, RB_DEV).astype(jnp.int32)
    slots_other = jax.random.randint(jax.random.fold_in(key, 13), (STEPS,), 0, RB_DEV).astype(jnp.int32)
    slots_second = jnp.where(step_ids == 0, 0, jnp.where(step_ids == STEPS - 1, RB_DEV - 1, slots_other)).astype(jnp.int32)
    firsts = (slots_first * N_PROW + owner_first).astype(jnp.int32)
    seconds = (slots_second * N_PROW + owner_second).astype(jnp.int32)
    others = jax.random.permutation(jax.random.fold_in(key, 12), NC - 1)[:STEPS - 1]
    cols = jnp.concatenate([others.astype(jnp.int32), jnp.full((1,), NC - 1, jnp.int32)])
    return jnp.stack([firsts, seconds, cols], axis=1).astype(jnp.int32)


def with_ends(result, stream_key, low, largest):
    longest = result.shape.index(max(result.shape))
    spots = []
    for shift in (0, 1):
        where = [jax.random.randint(jax.random.fold_in(stream_key, axis), (), 0, length) for axis, length in enumerate(result.shape)]
        where[longest] = (where[longest] + shift) % result.shape[longest]
        spots.append(tuple(where))
    return result.at[spots[0]].set(low).at[spots[1]].set(largest)


def block_levels(rng, shape, cuts, least, largest):
    loudness, own = 1.0, jax.random.fold_in(rng, 6)
    for position, blocks in cuts:
        heights = jnp.exp(jax.random.uniform(jax.random.fold_in(own, position), (blocks,), jnp.float32, least / len(cuts), largest / len(cuts)))
        loudness = loudness * jnp.repeat(heights, shape[position] // blocks).reshape([-1 if axis == position else 1 for axis in range(len(shape))])
    return loudness


def centred(stream_key, extent, spread, most, pieces=(), held_as=jnp.bfloat16):
    drawn = spread * jax.random.normal(stream_key, extent, jnp.float32)
    if pieces:
        drawn = drawn * block_levels(stream_key, extent, pieces, -0.22, 0.18)
    return jnp.clip(drawn, -most, most).astype(held_as)


def setup_inputs(seed: int = 0) -> dict:
    key_list = jax.random.split(jax.random.key(seed), 5)
    matrix = centred(key_list[0], (RB_DEV, NB * N_PROW, CB_DEV, NB * N_PCOL), 1.0, 6.0, ((1, 16), (3, 32)))
    pattern = with_ends((jax.random.randint(key_list[1], (MB, NC), 0, 4) < 3).astype(jnp.int32), jax.random.fold_in(key_list[1], 1), 0, 1)
    inverses = centred(key_list[2], (STEPS, NB, NB), (NB * NB) ** -0.5, 0.01171875)
    pivots = draw_pivots(jax.random.fold_in(key_list[4], 71), 0)
    return {"matrix": matrix, "pattern": pattern, "inverses": inverses, "pivots": pivots}


def reference(matrix, pattern, inverses, pivots):
    blocks = matrix.reshape(MB, NB, NC, NB)
    keep = pattern.astype(matrix.dtype)
    work = blocks * keep[:, None, :, None]
    row_ids = jnp.arange(MB, dtype=jnp.int32)
    col_ids = jnp.arange(NC, dtype=jnp.int32)
    for step in range(STEPS):
        first = pivots[step, 0]
        second = pivots[step, 1]
        column_id = pivots[step, 2]
        row_first = work[first]
        row_second = work[second]
        work = work.at[first].set(row_second)
        work = work.at[second].set(row_first)
        column = work[:, :, column_id, :]
        multipliers = jnp.dot(column.reshape(MB * NB, NB), inverses[step], preferred_element_type=jnp.float32)
        multipliers = multipliers.astype(matrix.dtype).reshape(MB, NB, NB)
        upper = work[first].reshape(NB, NC * NB)
        live_rows = jnp.all(row_ids[:, None] != pivots[None, :step + 1, 0], axis=1)
        live_cols = jnp.all(col_ids[:, None] != pivots[None, :step + 1, 2], axis=1)
        is_column = col_ids == column_id

        def update(item):
            old, left, live = item
            product = jnp.dot(left, upper, preferred_element_type=jnp.float32).reshape(NB, NC, NB)
            fresh = (old.astype(jnp.float32) - product).astype(matrix.dtype)
            mixed = jnp.where(live_cols[None, :, None], fresh, jnp.where(is_column[None, :, None], left[:, None, :], old))
            return jnp.where(live, mixed, old)

        work = lax.map(update, (work, multipliers, live_rows))
    return work.reshape(RB_DEV, NB * N_PROW, CB_DEV, NB * N_PCOL)
```

```python
import jax
import jax.numpy as jnp
from jax import lax
from jax.experimental import pallas as pl
from jax.experimental.pallas import tpu as pltpu
from jax.sharding import PartitionSpec as P

BF = jnp.bfloat16
F32 = jnp.float32
MESH = pl.DeviceIdType.MESH
PIECE = 16
CHUNK = 32
WINDOW = 2


def gather(piv, m, pn, xn, rr, sw, *scratch):
    (a1_0, a1_1, a1_2, q_0, q_1, q_2, a2_0, a2_1, a2_2, s_0, s_1, s_2, lp, w, wsrc, swsrc,
     a1_send, a1_recv, a2_send, a2_recv, g1_send, g1_recv, g1_loc, g2_send, g2_recv, g3_send, g3_recv,
     d_send, d_recv, r_send, r_edge, r_recv, r_loc, l_send, l_edge, l_recv,
     sw_send, sw_recv, w_send, w_recv, tok_up, tok_down) = scratch
    a1, q, a2, s_ = (a1_0, a1_1, a1_2), (q_0, q_1, q_2), (a2_0, a2_1, a2_2), (s_0, s_1, s_2)
    size = m.shape[1]
    half, quarter = size // 2, size // 8
    n_chunk = size // CHUNK
    z = lax.axis_index("prow")
    p = lax.axis_index("pcol")
    nz = lax.axis_size("prow")
    mid = nz // 2
    last = nz - 1
    x, y, k = p >> 3, (p >> 1) & 3, p & 1
    f, g = jnp.where(k == 0, x, y), jnp.where(k == 0, y, x)
    low = z < mid
    edge = jnp.logical_or(z == 0, z == last)
    first_one = piv[0, 1] == 0

    def dev(ff, gg):
        xx, yy = jnp.where(k == 0, ff, gg), jnp.where(k == 0, gg, ff)
        return {"pcol": xx * 8 + yy * 2 + k}

    partner = {"pcol": p ^ 1}

    def rc(src, dst, send, recv, device):
        return pltpu.make_async_remote_copy(
            src_ref=src, dst_ref=dst, send_sem=send, recv_sem=recv, device_id=device, device_id_type=MESH
        )

    def rows(start, count, align):
        return pl.ds(pl.multiple_of(start, align), count)

    barrier = pltpu.get_barrier_semaphore()
    mates = [partner]
    for t in (1, 2, 3):
        for kk in (0, 1):
            mates.append({"pcol": ((x + t) & 3) * 8 + y * 2 + kk})
            mates.append({"pcol": x * 8 + ((y + t) & 3) * 2 + kk})
    mates.append({"prow": (z + 1) & last})
    mates.append({"prow": (z + last) & last})
    for mate in mates:
        pl.semaphore_signal(barrier, inc=1, device_id=mate, device_id_type=MESH)
    pl.semaphore_wait(barrier, len(mates))

    def slot_of(o):
        return jnp.where(low, o, 2 - o)

    a1_sends = []

    def start_a1(o):
        slot = slot_of(o)
        own = pltpu.make_async_copy(
            m.at[slot, rows(k * half + f * quarter, quarter, quarter), :],
            a1[o].at[f * 2 + k], a1_recv.at[o, f * 2 + k],
        )
        own.start()
        copy = rc(
            m.at[slot, rows((1 - k) * half + g * quarter, quarter, quarter), :],
            a1[o].at[g * 2 + k], a1_send.at[o, 0], a1_recv.at[o, g * 2 + k], partner,
        )
        copy.start()
        a1_sends.append(copy)
        for t in (2, 1, 3):
            x2, y2 = (x + t) & 3, (y + t) & 3
            for n, (pos, here, target) in enumerate(
                ((x2, x, x2 * 8 + y * 2), (y2, y, x * 8 + y2 * 2 + 1))
            ):
                copy = rc(
                    m.at[slot, rows(n * half + pos * quarter, quarter, quarter), :],
                    a1[o].at[here * 2 + k], a1_send.at[o, 2 * t + n - 1],
                    a1_recv.at[o, here * 2 + k], {"pcol": target},
                )
                copy.start()
                a1_sends.append(copy)

    def finish_a1(o):
        def take(j):
            return rc(a1[o].at[j], a1[o].at[j], a1_send.at[o, 0], a1_recv.at[o, j], partner)

        pltpu.make_async_copy(a1[o].at[f * 2 + k], a1[o].at[f * 2 + k], a1_recv.at[o, f * 2 + k]).wait()
        take(f * 2 + 1 - k).wait_recv()
        for t in (1, 3, 2):
            for kk in (0, 1):
                take(((f + t) & 3) * 2 + kk).wait_recv()
        for ci in (0, 1):
            c = piv[ci, 2]
            place = jnp.where(k == 0, c >> 3, (c >> 1) & 3) * 2 + (c & 1)
            q[o][ci] = a1[o][place]

    a2_sends = []

    def start_a2(o):
        a2[o][g] = q[o][:, rows(g * PIECE, PIECE, PIECE), :]
        for t in (2, 1, 3):
            g2 = (g + t) & 3
            copy = rc(
                q[o].at[:, rows(g2 * PIECE, PIECE, PIECE), :], a2[o].at[g],
                a2_send.at[o, t - 1], a2_recv.at[o, g], dev(f, g2),
            )
            copy.start()
            a2_sends.append(copy)

    def finish_a2(o):
        for t in (1, 3, 2):
            j = (g + t) & 3
            rc(a2[o].at[j], a2[o].at[j], a2_send.at[o, 0], a2_recv.at[o, j], partner).wait_recv()
        for ci in (0, 1):
            c = piv[ci, 2]
            place = jnp.where(k == 0, (c >> 1) & 3, c >> 3)
            s_[o][ci] = a2[o][place, ci]

    base = k * half + f * quarter

    def dst(u, where):
        if u == 3:
            return xn.at[:, where, :]
        return pn.at[:, slot_of(u), where, :]

    def piece(u):
        return (w, s_[1], s_[2], lp)[u]

    def spot(ff, gg):
        return rows(k * half + ff * quarter + gg * PIECE, PIECE, PIECE)

    g_sends = []

    def start_g1(u):
        pltpu.make_async_copy(piece(u), dst(u, spot(f, g)), g1_loc.at[u]).start()
        for t in (2, 1, 3):
            copy = rc(
                piece(u), dst(u, spot(f, g)), g1_send.at[u, t - 1], g1_recv.at[u, g], dev(f, (g + t) & 3)
            )
            copy.start()
            g_sends.append(copy)

    def start_g2(u):
        pltpu.make_async_copy(piece(u), dst(u, spot(f, g)), g1_loc.at[u]).wait()
        for t in (1, 3, 2):
            j = (g + t) & 3
            rc(piece(u), dst(u, spot(f, j)), g1_send.at[u, 0], g1_recv.at[u, j], partner).wait_recv()
        for n, step in enumerate((1, 3)):
            block = dst(u, rows(base, quarter, quarter))
            copy = rc(block, block, g2_send.at[u, n], g2_recv.at[u, n], dev((f + step) & 3, g))
            copy.start()
            g_sends.append(copy)

    def start_g3(u):
        for n, step in enumerate((1, 3)):
            source = (f + 4 - step) & 3
            block = dst(u, rows(k * half + source * quarter, quarter, quarter))
            rc(block, block, g2_send.at[u, n], g2_recv.at[u, n], partner).wait_recv()
            part = dst(u, rows(k * half + source * quarter + n * (quarter // 2), quarter // 2, quarter // 2))
            copy = rc(part, part, g3_send.at[u, n], g3_recv.at[u, n], dev((f + step) & 3, g))
            copy.start()
            g_sends.append(copy)

    def start_d(u):
        across = (f + 2) & 3
        for n in (0, 1):
            part = dst(u, rows(k * half + across * quarter + n * (quarter // 2), quarter // 2, quarter // 2))
            rc(part, part, g3_send.at[u, n], g3_recv.at[u, n], partner).wait_recv()
        block = dst(u, rows(k * half, half, half))
        copy = rc(block, block, d_send.at[u], d_recv.at[u], partner)
        copy.start()
        g_sends.append(copy)

    def finish_d(u):
        block = dst(u, rows((1 - k) * half, half, half))
        rc(block, block, d_send.at[u], d_recv.at[u], partner).wait_recv()

    child = {"prow": jnp.where(low, z + 1, z - 1) & last}
    other_edge = {"prow": last - z}
    has_child = jnp.logical_and(z != mid - 1, z != mid)

    def chain_copies(b, i):
        block = rr.at[b, rows(i * CHUNK, CHUNK, CHUNK), :]
        down = rc(block, block, r_send.at[b, i], r_recv.at[b, i], child)
        over = rc(block, block, r_edge.at[i], r_recv.at[b, i], other_edge)
        return down, over

    def chain_step(i, carry):
        for b in (0, 1):
            down, over = chain_copies(b, i)
            own = z == (0 if b == 0 else last)

            @pl.when(own)
            def _():
                over.start()

            @pl.when(jnp.logical_not(own))
            def _():
                down.wait_recv()

            @pl.when(has_child)
            def _():
                down.start()

        for b in (0, 1):
            down, over = chain_copies(b, jnp.maximum(i - WINDOW, 0))
            own = z == (0 if b == 0 else last)

            @pl.when(jnp.logical_and(i >= WINDOW, has_child))
            def _():
                down.wait_send()

            @pl.when(jnp.logical_and(i >= WINDOW, own))
            def _():
                over.wait_send()

        return carry

    def chain(lo, hi):
        lax.fori_loop(lo, hi, chain_step, 0)

    def corner(b):
        down = rc(lp.at[b], lp.at[b], l_send.at[b], l_recv.at[b], child)
        over = rc(lp.at[b], lp.at[b], l_edge, l_recv.at[b], other_edge)
        return down, over

    def relay_corners():
        for b in (0, 1):
            down, over = corner(b)
            own = z == (0 if b == 0 else last)

            @pl.when(own)
            def _():
                over.start()

            @pl.when(jnp.logical_not(own))
            def _():
                down.wait_recv()

            @pl.when(has_child)
            def _():
                down.start()

    for o in (0, 1, 2):
        start_a1(o)

    @pl.when(edge)
    def _():
        b = jnp.where(z == 0, 0, 1)
        copy = pltpu.make_async_copy(m.at[jnp.where(z == 0, 0, 2)], rr.at[b], r_loc)
        copy.start()
        copy.wait()

    give = jnp.logical_or(z == mid, z == mid - 1)
    slot_a = jnp.where(jnp.logical_xor(z == mid, first_one), piv[1, 0], piv[0, 0]) >> 4

    @pl.when(z == 0)
    def _():
        pl.semaphore_signal(tok_up, inc=1, device_id={"prow": z + 1}, device_id_type=MESH)

    @pl.when(z == last)
    def _():
        pl.semaphore_signal(tok_down, inc=1, device_id={"prow": z - 1}, device_id_type=MESH)

    @pl.when(jnp.logical_and(z >= 1, z <= mid))
    def _():
        pl.semaphore_wait(tok_up, 1)

    @pl.when(jnp.logical_and(z >= 1, z < mid))
    def _():
        pl.semaphore_signal(tok_up, inc=1, device_id={"prow": z + 1}, device_id_type=MESH)

    @pl.when(jnp.logical_and(z >= mid - 1, z < last))
    def _():
        pl.semaphore_wait(tok_down, 1)

    @pl.when(jnp.logical_and(z >= mid, z < last))
    def _():
        pl.semaphore_signal(tok_down, inc=1, device_id={"prow": z - 1}, device_id_type=MESH)

    receiver = {"prow": jnp.where(z == mid, 0, last)}
    sw_copy = rc(swsrc, sw, sw_send, sw_recv, receiver)
    w_copy = rc(wsrc, w, w_send, w_recv, receiver)

    @pl.when(give)
    def _():
        swsrc[...] = m[slot_a]
        sw_copy.start()

    far = jnp.where(low, z, last - z)

    def at(us):
        return jnp.clip((us * 10 - far * 14) // 14, 0, n_chunk)

    marks = [at(us) for us in (5, 8, 11, 14, 17)]
    chain(0, marks[0])
    finish_a1(0)
    start_a2(0)
    chain(marks[0], marks[1])
    finish_a1(1)
    start_a2(1)
    finish_a2(0)

    @pl.when(edge)
    def _():
        which = jnp.where(jnp.logical_xor(z == 0, first_one), 0, 1)
        lp[jnp.where(z == 0, 0, 1)] = s_[0][which]

    chain(marks[1], marks[2])
    finish_a1(2)
    start_a2(2)
    finish_a2(1)
    start_g1(1)

    @pl.when(jnp.logical_not(give))
    def _():
        relay_corners()

    chain(marks[2], marks[3])
    finish_a2(2)
    start_g1(2)

    @pl.when(give)
    def _():
        order_a = jnp.where(z == mid, 2 - slot_a, slot_a)
        value = jnp.where(order_a == 1, s_[1][...], s_[0][...])
        wsrc[...] = jnp.where(order_a == 2, s_[2][...], value)
        w_copy.start()

    @pl.when(give)
    def _():
        relay_corners()

    start_g2(1)
    start_g1(3)
    chain(marks[3], marks[4])
    start_g2(2)
    start_g3(1)

    @pl.when(edge)
    def _():
        w_copy.wait_recv()

    @pl.when(jnp.logical_not(edge))
    def _():
        w[...] = s_[0][...]

    start_g1(0)
    start_g2(3)
    start_g3(2)
    start_d(1)
    start_g2(0)
    start_g3(3)
    start_d(2)
    start_g3(0)
    start_d(3)
    chain(marks[4], n_chunk)
    start_d(0)
    for u in (1, 2, 3, 0):
        finish_d(u)

    @pl.when(edge)
    def _():
        sw_copy.wait_recv()

    @pl.when(give)
    def _():
        sw_copy.wait_send()
        w_copy.wait_send()

    for copy in a1_sends + a2_sends + g_sends:
        copy.wait_send()
    for b in (0, 1):
        own = z == (0 if b == 0 else last)
        down, over = corner(b)

        @pl.when(has_child)
        def _():
            down.wait_send()
            for i in range(n_chunk - WINDOW, n_chunk):
                chain_copies(b, i)[0].wait_send()

        @pl.when(own)
        def _():
            over.wait_send()
            for i in range(n_chunk - WINDOW, n_chunk):
                chain_copies(b, i)[1].wait_send()


def run_gather(pivots, blocks):
    slots, size, width = blocks.shape
    n_chunk = size // CHUNK
    quarter = size // 8
    vm = pltpu.VMEM
    dma = pltpu.SemaphoreType.DMA
    scratch = (
        [vm((8, quarter, width), BF)] * 3
        + [vm((2, quarter, width), BF)] * 3
        + [vm((4, 2, PIECE, width), BF)] * 3
        + [vm((2, PIECE, width), BF)] * 6
        + [vm((size, width), BF)]
        + [dma((3, 8)), dma((3, 8)), dma((3, 3)), dma((3, 4)), dma((4, 3)), dma((4, 4)), dma((4,))]
        + [dma((4, 2)), dma((4, 2)), dma((4, 2)), dma((4, 2)), dma((4,)), dma((4,))]
        + [dma((2, n_chunk)), dma((n_chunk,)), dma((2, n_chunk)), dma(())]
        + [dma((2,)), dma(()), dma((2,))]
        + [dma(())] * 4
        + [pltpu.SemaphoreType.REGULAR] * 2
    )
    return pl.pallas_call(
        gather,
        out_shape=[
            jax.ShapeDtypeStruct((2, slots, size, width), BF),
            jax.ShapeDtypeStruct((2, size, width), BF),
            jax.ShapeDtypeStruct((2, size, width), BF),
            jax.ShapeDtypeStruct((size, width), BF),
        ],
        in_specs=[pl.BlockSpec(memory_space=pltpu.SMEM), pl.BlockSpec(memory_space=pltpu.VMEM)],
        out_specs=[pl.BlockSpec(memory_space=pltpu.VMEM)] * 4,
        scratch_shapes=scratch,
        compiler_params=pltpu.CompilerParams(collective_id=0, has_side_effects=True),
        name="gather",
    )(pivots, blocks)


def local(matrix, pattern, inverses, pivots):
    nrow = lax.axis_size("prow")
    slots, size, _, width = matrix.shape
    my_row = lax.axis_index("prow")
    my_col = lax.axis_index("pcol")
    blocks = matrix.reshape(slots, size, width)
    panels, corners, tops, swapped = run_gather(pivots, blocks)
    a1, b1, c1 = pivots[0, 0], pivots[0, 1], pivots[0, 2]
    a2, b2, c2 = pivots[1, 0], pivots[1, 1], pivots[1, 2]
    low_first = b1 == 0
    ids = jnp.arange(slots, dtype=jnp.int32) * nrow + my_row
    held = jnp.where(ids == b1, a1, jnp.where(ids == b2, a2, ids))
    taken = ids != held
    keep = pattern.astype(BF)
    work = jnp.where(taken[:, None, None], swapped[None], blocks) * keep[held, my_col][:, None, None]
    panel1 = panels[0] * keep[held, c1][:, None, None]
    panel2 = panels[1] * keep[held, c2][:, None, None]
    corner12 = jnp.where(low_first, corners[0], corners[1]) * keep[b1, c2]
    corner21 = jnp.where(low_first, corners[1], corners[0]) * keep[b2, c1]
    upper1 = jnp.where(low_first, tops[0], tops[1]) * keep[b1, my_col]
    raw2 = jnp.where(low_first, tops[1], tops[0]) * keep[b2, my_col]

    def dot(left, right):
        return jnp.dot(left, right, preferred_element_type=F32)

    def less(old, left, right):
        return (old.astype(F32) - dot(left, right)).astype(BF)

    flat = (slots * size, width)
    left1 = dot(panel1.reshape(flat), inverses[0]).astype(BF)
    top_left = dot(corner21, inverses[0]).astype(BF)
    upper2 = jnp.where(my_col == c1, top_left, less(raw2, top_left, upper1))
    step1 = less(work.reshape(flat), left1, upper1)
    panel2 = less(panel2.reshape(flat), left1, corner12)
    left2 = dot(panel2, inverses[1]).astype(BF)
    step2 = less(step1, left2, upper2)
    mixed = jnp.where(my_col == c1, left1, jnp.where(my_col == c2, left2, step2)).reshape(blocks.shape)
    is1, is2 = (ids == a1)[:, None, None], (ids == a2)[:, None, None]
    out = jnp.where(is1, upper1[None], jnp.where(is2, upper2[None], mixed))
    return out.reshape(matrix.shape)


def solution(mesh):
    placed = (P(None, "prow", None, "pcol"), P(), P(), P())
    return jax.shard_map(
        local, mesh=mesh, in_specs=placed, out_specs=P(None, "prow", None, "pcol"), check_vma=False
    )
```

```python
import jax
import jax.numpy as jnp
from jax import lax
from jax.experimental import pallas as pl
from jax.experimental.pallas import tpu as pltpu
from jax.sharding import PartitionSpec as P

BF = jnp.bfloat16
F32 = jnp.float32
MESH = pl.DeviceIdType.MESH
PIECE = 16
CHUNK = 32


def gather(piv, m, pn, xn, rr, sw, *scratch):
    (a1_0, a1_1, a1_2, q_0, q_1, q_2, a2_0, a2_1, a2_2, s_0, s_1, s_2, lp, w, wsrc, swsrc,
     a1_send, a1_recv, a2_send, a2_recv, g1_send, g1_recv, g1_loc, g2_send, g2_recv,
     d_send, d_recv, r_send, r_recv, r_loc, l_send, l_recv,
     sw_send, sw_recv, w_send, w_recv, tok_up, tok_down, tok_in, tok_over) = scratch
    a1, q, a2, s_ = (a1_0, a1_1, a1_2), (q_0, q_1, q_2), (a2_0, a2_1, a2_2), (s_0, s_1, s_2)
    size = m.shape[1]
    half, quarter = size // 2, size // 8
    n_chunk = size // CHUNK
    z = lax.axis_index("prow")
    p = lax.axis_index("pcol")
    nz = lax.axis_size("prow")
    mid = nz // 2
    last = nz - 1
    x, y, k = p >> 3, (p >> 1) & 3, p & 1
    f, g = jnp.where(k == 0, x, y), jnp.where(k == 0, y, x)
    low = z < mid
    edge = jnp.logical_or(z == 0, z == last)
    first_one = piv[0, 1] == 0

    def dev(ff, gg):
        xx, yy = jnp.where(k == 0, ff, gg), jnp.where(k == 0, gg, ff)
        return {"pcol": xx * 8 + yy * 2 + k}

    partner = {"pcol": p ^ 1}

    def rc(src, dst, send, recv, device):
        return pltpu.make_async_remote_copy(
            src_ref=src, dst_ref=dst, send_sem=send, recv_sem=recv, device_id=device, device_id_type=MESH
        )

    def rows(start, count, align):
        return pl.ds(pl.multiple_of(start, align), count)

    barrier = pltpu.get_barrier_semaphore()
    mates = [partner]
    for t in (1, 2, 3):
        for kk in (0, 1):
            mates.append({"pcol": ((x + t) & 3) * 8 + y * 2 + kk})
            mates.append({"pcol": x * 8 + ((y + t) & 3) * 2 + kk})
    mates.append({"prow": (z + 1) & last})
    mates.append({"prow": (z + last) & last})
    for mate in mates:
        pl.semaphore_signal(barrier, inc=1, device_id=mate, device_id_type=MESH)
    hub = mid // 2

    @pl.when(jnp.logical_or(z == hub, z == last - hub))
    def _():
        for at in (0, last):
            pl.semaphore_signal(barrier, inc=1, device_id={"prow": at}, device_id_type=MESH)

    pl.semaphore_wait(barrier, jnp.where(edge, len(mates) + 2, len(mates)))

    def slot_of(o):
        return jnp.where(low, o, 2 - o)

    a1_sends = []

    def start_a1(o):
        slot = slot_of(o)
        own = pltpu.make_async_copy(
            m.at[slot, rows(k * half + f * quarter, quarter, quarter), :],
            a1[o].at[f * 2 + k], a1_recv.at[o, f * 2 + k],
        )
        own.start()
        copy = rc(
            m.at[slot, rows((1 - k) * half + g * quarter, quarter, quarter), :],
            a1[o].at[g * 2 + k], a1_send.at[o, 0], a1_recv.at[o, g * 2 + k], partner,
        )
        copy.start()
        a1_sends.append(copy)
        for t in (2, 1, 3):
            x2, y2 = (x + t) & 3, (y + t) & 3
            for n, (pos, here, target) in enumerate(
                ((x2, x, x2 * 8 + y * 2), (y2, y, x * 8 + y2 * 2 + 1))
            ):
                copy = rc(
                    m.at[slot, rows(n * half + pos * quarter, quarter, quarter), :],
                    a1[o].at[here * 2 + k], a1_send.at[o, 2 * t + n - 1],
                    a1_recv.at[o, here * 2 + k], {"pcol": target},
                )
                copy.start()
                a1_sends.append(copy)

    def finish_a1(o):
        def take(j):
            return rc(a1[o].at[j], a1[o].at[j], a1_send.at[o, 0], a1_recv.at[o, j], partner)

        pltpu.make_async_copy(a1[o].at[f * 2 + k], a1[o].at[f * 2 + k], a1_recv.at[o, f * 2 + k]).wait()
        take(f * 2 + 1 - k).wait_recv()
        for t in (1, 3, 2):
            for kk in (0, 1):
                take(((f + t) & 3) * 2 + kk).wait_recv()
        for ci in (0, 1):
            c = piv[ci, 2]
            place = jnp.where(k == 0, c >> 3, (c >> 1) & 3) * 2 + (c & 1)
            q[o][ci] = a1[o][place]

    a2_sends = []

    def start_a2(o):
        a2[o][g] = q[o][:, rows(g * PIECE, PIECE, PIECE), :]
        for t in (2, 1, 3):
            g2 = (g + t) & 3
            copy = rc(
                q[o].at[:, rows(g2 * PIECE, PIECE, PIECE), :], a2[o].at[g],
                a2_send.at[o, t - 1], a2_recv.at[o, g], dev(f, g2),
            )
            copy.start()
            a2_sends.append(copy)

    def finish_a2(o):
        for t in (1, 3, 2):
            j = (g + t) & 3
            rc(a2[o].at[j], a2[o].at[j], a2_send.at[o, 0], a2_recv.at[o, j], partner).wait_recv()
        for ci in (0, 1):
            c = piv[ci, 2]
            place = jnp.where(k == 0, (c >> 1) & 3, c >> 3)
            s_[o][ci] = a2[o][place, ci]

    base = k * half + f * quarter

    def dst(u, where):
        if u == 3:
            return xn.at[:, where, :]
        return pn.at[:, slot_of(u), where, :]

    def piece(u):
        return (w, s_[1], s_[2], lp)[u]

    def spot(ff, gg):
        return rows(k * half + ff * quarter + gg * PIECE, PIECE, PIECE)

    g_sends = []

    def start_g1(u):
        pltpu.make_async_copy(piece(u), dst(u, spot(f, g)), g1_loc.at[u]).start()
        for t in (2, 1, 3):
            copy = rc(
                piece(u), dst(u, spot(f, g)), g1_send.at[u, t - 1], g1_recv.at[u, g], dev(f, (g + t) & 3)
            )
            copy.start()
            g_sends.append(copy)

    def start_g2(u):
        pltpu.make_async_copy(piece(u), dst(u, spot(f, g)), g1_loc.at[u]).wait()
        for t in (1, 3, 2):
            j = (g + t) & 3
            rc(piece(u), dst(u, spot(f, j)), g1_send.at[u, 0], g1_recv.at[u, j], partner).wait_recv()
        block = dst(u, rows(base, quarter, quarter))
        for t in (2, 1, 3):
            copy = rc(block, block, g2_send.at[u, t - 1], g2_recv.at[u, f], dev((f + t) & 3, g))
            copy.start()
            g_sends.append(copy)

    def start_d(u):
        for t in (1, 3, 2):
            j = (f + t) & 3
            block = dst(u, rows(k * half + j * quarter, quarter, quarter))
            rc(block, block, g2_send.at[u, 0], g2_recv.at[u, j], partner).wait_recv()
        block = dst(u, rows(k * half, half, half))
        copy = rc(block, block, d_send.at[u], d_recv.at[u], partner)
        copy.start()
        g_sends.append(copy)

    def finish_d(u):
        block = dst(u, rows((1 - k) * half, half, half))
        rc(block, block, d_send.at[u], d_recv.at[u], partner).wait_recv()

    h = jnp.where(low, z, last - z)

    def at_height(height):
        return {"prow": jnp.where(low, height, last - height) & last}

    other_edge = {"prow": last - z}
    relays = jnp.logical_and(h >= 2, h <= mid - 2)
    sinks = jnp.logical_and(h >= 2, h <= hub)
    rises = jnp.logical_and(h >= hub, h <= mid - 2)

    def row_chunk(b, i, n, device):
        block = rr.at[b, rows(i * CHUNK, CHUNK, CHUNK), :]
        return rc(block, block, r_send.at[n, b, i], r_recv.at[b, i], device)

    def source_copies(b, i):
        return (
            row_chunk(b, i, 0, {"prow": hub}),
            row_chunk(b, i, 1, {"prow": last - hub}),
            row_chunk(b, i, 2, other_edge),
        )

    def relay_step(i, carry):
        for b in (0, 1):
            fall, rise = row_chunk(b, i, 0, at_height(h - 1)), row_chunk(b, i, 1, at_height(h + 1))
            fall.wait_recv()

            @pl.when(sinks)
            def _():
                fall.start()

            @pl.when(rises)
            def _():
                rise.start()

        return carry

    def chain(lo, hi):
        lax.fori_loop(lo, hi, relay_step, 0)

    def corner(b, t):
        return rc(lp.at[b], lp.at[b], l_send.at[t - 1], l_recv.at[b], {"prow": (z + t) & last})

    for o in (0, 1, 2):
        start_a1(o)

    for b, at in ((0, 0), (1, last)):

        @pl.when(z == at)
        def _():
            copy = pltpu.make_async_copy(m.at[0 if b == 0 else 2], rr.at[b], r_loc)
            copy.start()
            copy.wait()

            def send(i, carry):
                for copy in source_copies(b, i):
                    copy.start()
                return carry

            lax.fori_loop(0, n_chunk, send, 0)

    give = jnp.logical_or(z == mid, z == mid - 1)
    slot_a = jnp.where(jnp.logical_xor(z == mid, first_one), piv[1, 0], piv[0, 0]) >> 4

    @pl.when(z == 0)
    def _():
        pl.semaphore_signal(tok_up, inc=1, device_id={"prow": z + 1}, device_id_type=MESH)

    @pl.when(z == last)
    def _():
        pl.semaphore_signal(tok_down, inc=1, device_id={"prow": z - 1}, device_id_type=MESH)

    @pl.when(jnp.logical_and(z >= 1, z <= mid))
    def _():
        pl.semaphore_wait(tok_up, 1)

    @pl.when(jnp.logical_and(z >= 1, z < mid))
    def _():
        pl.semaphore_signal(tok_up, inc=1, device_id={"prow": z + 1}, device_id_type=MESH)

    @pl.when(jnp.logical_and(z >= mid - 1, z < last))
    def _():
        pl.semaphore_wait(tok_down, 1)

    @pl.when(jnp.logical_and(z >= mid, z < last))
    def _():
        pl.semaphore_signal(tok_down, inc=1, device_id={"prow": z - 1}, device_id_type=MESH)

    receiver = {"prow": jnp.where(z == mid, 0, last)}
    sw_copy = rc(swsrc, sw, sw_send, sw_recv, receiver)
    w_copy = rc(wsrc, w, w_send, w_recv, receiver)

    @pl.when(give)
    def _():
        swsrc[...] = m[slot_a]
        sw_copy.start()

    begin = 90 + 33 * jnp.abs(h - hub)

    def mark(us):
        return jnp.where(relays, jnp.clip(jnp.maximum(us * 10 - begin, 0) // 12, 0, n_chunk), 0)

    marks = [mark(us) for us in (9, 12, 14, 18, 20, 22, 25, 27, 29, 33)]
    done = [0]

    def relay_to(n):
        chain(done[-1], marks[n])
        done.append(marks[n])

    relay_to(0)
    finish_a1(0)
    start_a2(0)

    @pl.when(jnp.logical_and(h >= 1, h < mid - 1))
    def _():
        pl.semaphore_wait(tok_in, 1)

    @pl.when(h >= 1)
    def _():
        pl.semaphore_signal(tok_in, inc=1, device_id=at_height(h - 1), device_id_type=MESH)

    relay_to(1)
    finish_a1(1)
    start_a2(1)
    finish_a2(0)

    @pl.when(edge)
    def _():
        which = jnp.where(jnp.logical_xor(z == 0, first_one), 0, 1)
        lp[jnp.where(z == 0, 0, 1)] = s_[0][which]
        pl.semaphore_wait(tok_in, 1)
        pl.semaphore_signal(tok_over, inc=1, device_id=other_edge, device_id_type=MESH)
        pl.semaphore_wait(tok_over, 1)

    for b, at in ((0, 0), (1, last)):

        @pl.when(z == at)
        def _():
            for t in (8, 7, 9, 6, 10, 5, 11, 4, 12, 3, 13, 2, 14, 1, 15):
                corner(b, t).start()

    relay_to(2)
    finish_a1(2)
    start_a2(2)
    finish_a2(1)
    start_g1(1)
    relay_to(3)
    finish_a2(2)

    @pl.when(give)
    def _():
        order_a = jnp.where(z == mid, 2 - slot_a, slot_a)
        value = jnp.where(order_a == 1, s_[1][...], s_[0][...])
        wsrc[...] = jnp.where(order_a == 2, s_[2][...], value)
        w_copy.start()

    start_g1(2)
    relay_to(4)
    start_g2(1)
    relay_to(5)
    for b, at in ((0, 0), (1, last)):

        @pl.when(z != at)
        def _():
            corner(b, 1).wait_recv()

    start_g1(3)
    start_g2(2)
    relay_to(6)
    start_d(1)
    relay_to(7)

    @pl.when(edge)
    def _():
        w_copy.wait_recv()

    @pl.when(jnp.logical_not(edge))
    def _():
        w[...] = s_[0][...]

    start_g1(0)
    start_g2(3)
    relay_to(8)
    start_d(2)
    start_g2(0)
    relay_to(9)
    start_d(3)
    chain(done[-1], jnp.where(relays, n_chunk, 0))
    start_d(0)
    for u in (1, 2, 3, 0):
        finish_d(u)

    @pl.when(edge)
    def _():
        sw_copy.wait_recv()

    def leaf(i, carry):
        for b, at in ((0, 0), (1, last)):

            @pl.when(z != at)
            def _():
                row_chunk(b, i, 0, other_edge).wait_recv()

        return carry

    lax.fori_loop(0, jnp.where(relays, 0, n_chunk), leaf, 0)

    @pl.when(give)
    def _():
        sw_copy.wait_send()
        w_copy.wait_send()

    for copy in a1_sends + a2_sends + g_sends:
        copy.wait_send()

    for b, at in ((0, 0), (1, last)):

        @pl.when(z == at)
        def _():
            for t in range(1, 16):
                corner(b, t).wait_send()

            def sent(i, carry):
                for copy in source_copies(b, i):
                    copy.wait_send()
                return carry

            lax.fori_loop(0, n_chunk, sent, 0)

    def relayed(i, carry):
        for b in (0, 1):

            @pl.when(sinks)
            def _():
                row_chunk(b, i, 0, other_edge).wait_send()

            @pl.when(rises)
            def _():
                row_chunk(b, i, 1, other_edge).wait_send()

        return carry

    lax.fori_loop(0, jnp.where(relays, n_chunk, 0), relayed, 0)


def run_gather(pivots, blocks):
    slots, size, width = blocks.shape
    n_chunk = size // CHUNK
    quarter = size // 8
    vm = pltpu.VMEM
    dma = pltpu.SemaphoreType.DMA
    scratch = (
        [vm((8, quarter, width), BF)] * 3
        + [vm((2, quarter, width), BF)] * 3
        + [vm((4, 2, PIECE, width), BF)] * 3
        + [vm((2, PIECE, width), BF)] * 6
        + [vm((size, width), BF)]
        + [dma((3, 8)), dma((3, 8)), dma((3, 3)), dma((3, 4)), dma((4, 3)), dma((4, 4)), dma((4,))]
        + [dma((4, 3)), dma((4, 4)), dma((4,)), dma((4,))]
        + [dma((3, 2, n_chunk)), dma((2, n_chunk)), dma(())]
        + [dma((15,)), dma((2,))]
        + [dma(())] * 4
        + [pltpu.SemaphoreType.REGULAR] * 4
    )
    return pl.pallas_call(
        gather,
        out_shape=[
            jax.ShapeDtypeStruct((2, slots, size, width), BF),
            jax.ShapeDtypeStruct((2, size, width), BF),
            jax.ShapeDtypeStruct((2, size, width), BF),
            jax.ShapeDtypeStruct((size, width), BF),
        ],
        in_specs=[pl.BlockSpec(memory_space=pltpu.SMEM), pl.BlockSpec(memory_space=pltpu.VMEM)],
        out_specs=[pl.BlockSpec(memory_space=pltpu.VMEM)] * 4,
        scratch_shapes=scratch,
        compiler_params=pltpu.CompilerParams(collective_id=0, has_side_effects=True),
        name="gather",
    )(pivots, blocks)


def update(piv, pat, blocks, panels, corners, tops, swapped, inv, out, lead, upper):
    slots, size, width = blocks.shape
    row = lax.axis_index("prow")
    col = lax.axis_index("pcol")
    nrow = lax.axis_size("prow")
    a1, b1, c1 = piv[0, 0], piv[0, 1], piv[0, 2]
    a2, b2, c2 = piv[1, 0], piv[1, 1], piv[1, 2]
    one = jnp.where(b1 == 0, 0, 1)
    two = 1 - one

    def keep(i, j):
        return pat[i, j].astype(F32)

    def dot(left, right):
        return jnp.dot(left, right, preferred_element_type=F32)

    own1 = keep(b1, col)
    cross12 = keep(b1, c2)
    lead[...] = (dot(corners[two], inv[0]) * keep(b2, c1)).astype(BF)

    @pl.when(col == c1)
    def _():
        upper[...] = lead[...]

    @pl.when(col != c1)
    def _():
        old = tops[two].astype(F32) * keep(b2, col)
        upper[...] = (old - dot(lead[...], tops[one]) * own1).astype(BF)

    def slot(s, carry):
        here = s * nrow + row
        held = jnp.where(here == b1, a1, jnp.where(here == b2, a2, here))
        old = jnp.where(here == held, blocks[s], swapped[...]).astype(F32) * keep(held, col)
        left1 = (dot(panels[0, s], inv[0]) * keep(held, c1)).astype(BF)
        step1 = (old - dot(left1, tops[one]) * own1).astype(BF)
        column2 = panels[1, s].astype(F32) * keep(held, c2) - dot(left1, corners[one]) * cross12
        left2 = dot(column2.astype(BF), inv[1]).astype(BF)
        out[s] = (step1.astype(F32) - dot(left2, upper[...])).astype(BF)

        @pl.when(col == c1)
        def _():
            out[s] = left1

        @pl.when(col == c2)
        def _():
            out[s] = left2

        @pl.when(here == a1)
        def _():
            out[s] = (tops[one].astype(F32) * own1).astype(BF)

        @pl.when(here == a2)
        def _():
            out[s] = upper[...]

        return carry

    lax.fori_loop(0, slots, slot, 0)


def run_update(pivots, pattern, blocks, panels, corners, tops, swapped, inverses):
    slots, size, width = blocks.shape
    smem, vmem = pl.BlockSpec(memory_space=pltpu.SMEM), pl.BlockSpec(memory_space=pltpu.VMEM)
    return pl.pallas_call(
        update,
        out_shape=jax.ShapeDtypeStruct(blocks.shape, BF),
        in_specs=[smem, smem] + [vmem] * 6,
        out_specs=vmem,
        scratch_shapes=[pltpu.VMEM((size, width), BF)] * 2,
        name="update",
    )(pivots, pattern, blocks, panels, corners, tops, swapped, inverses)


def local(matrix, pattern, inverses, pivots):
    slots, size, _, width = matrix.shape
    blocks = matrix.reshape(slots, size, width)
    moved = run_gather(pivots, blocks)
    return run_update(pivots, pattern, blocks, *moved, inverses).reshape(matrix.shape)


def solution(mesh):
    placed = (P(None, "prow", None, "pcol"), P(), P(), P())
    return jax.shard_map(
        local, mesh=mesh, in_specs=placed, out_specs=P(None, "prow", None, "pcol"), check_vma=False
    )
```

```python
import jax
import jax.numpy as jnp
from jax import lax
from jax.experimental import pallas as pl
from jax.experimental.pallas import tpu as pltpu
from jax.sharding import PartitionSpec as P

BF = jnp.bfloat16
F32 = jnp.float32
MESH = pl.DeviceIdType.MESH
PIECE = 16
CHUNK = 32
FIRST = 8


def gather(piv, m, pn, xn, rr, sw, *scratch):
    (a1_0, a1_1, a1_2, q_0, q_1, q_2, a2_0, a2_1, a2_2, s_0, s_1, s_2, lp, w, mp,
     a1_send, a1_recv, a2_send, a2_recv, g1_send, g1_recv, g1_loc, g2_send, g2_recv,
     d_send, d_recv, r_send, r_recv, r_loc, l_send, l_recv,
     sw_send, sw_recv, w_send, w_recv, tok_in, tok_out, tok_over, tok_go) = scratch
    a1, q, a2, s_ = (a1_0, a1_1, a1_2), (q_0, q_1, q_2), (a2_0, a2_1, a2_2), (s_0, s_1, s_2)
    size = m.shape[1]
    half, quarter = size // 2, size // 8
    n_chunk = size // CHUNK
    z = lax.axis_index("prow")
    p = lax.axis_index("pcol")
    nz = lax.axis_size("prow")
    mid = nz // 2
    last = nz - 1
    x, y, k = p >> 3, (p >> 1) & 3, p & 1
    f, g = jnp.where(k == 0, x, y), jnp.where(k == 0, y, x)
    low = z < mid
    edge = jnp.logical_or(z == 0, z == last)
    first_one = piv[0, 1] == 0

    def dev(ff, gg):
        xx, yy = jnp.where(k == 0, ff, gg), jnp.where(k == 0, gg, ff)
        return {"pcol": xx * 8 + yy * 2 + k}

    partner = {"pcol": p ^ 1}

    def rc(src, dst, send, recv, device):
        return pltpu.make_async_remote_copy(
            src_ref=src, dst_ref=dst, send_sem=send, recv_sem=recv, device_id=device, device_id_type=MESH
        )

    def rows(start, count, align):
        return pl.ds(pl.multiple_of(start, align), count)

    barrier = pltpu.get_barrier_semaphore()
    mates = [partner]
    for t in (1, 2, 3):
        for kk in (0, 1):
            mates.append({"pcol": ((x + t) & 3) * 8 + y * 2 + kk})
            mates.append({"pcol": x * 8 + ((y + t) & 3) * 2 + kk})
    mates.append({"prow": (z + 1) & last})
    mates.append({"prow": (z + last) & last})
    for mate in mates:
        pl.semaphore_signal(barrier, inc=1, device_id=mate, device_id_type=MESH)
    hub = mid // 2

    @pl.when(jnp.logical_or(z == hub, z == last - hub))
    def _():
        for at in (0, last):
            pl.semaphore_signal(barrier, inc=1, device_id={"prow": at}, device_id_type=MESH)

    pl.semaphore_wait(barrier, jnp.where(edge, len(mates) + 2, len(mates)))

    give = jnp.logical_or(z == mid, z == mid - 1)
    slot_a = jnp.where(jnp.logical_xor(z == mid, first_one), piv[1, 0], piv[0, 0]) >> 4
    for u in (0, 1, 2):
        turned = slot_a + u
        mp[u] = m[jnp.where(give, jnp.where(turned > 2, turned - 3, turned), jnp.where(low, u, 2 - u))]

    a1_sends = []

    def start_a1(o):
        own = pltpu.make_async_copy(
            mp.at[o, rows(k * half + f * quarter, quarter, quarter), :],
            a1[o].at[f * 2 + k], a1_recv.at[o, f * 2 + k],
        )
        own.start()
        copy = rc(
            mp.at[o, rows((1 - k) * half + g * quarter, quarter, quarter), :],
            a1[o].at[g * 2 + k], a1_send.at[o, 0], a1_recv.at[o, g * 2 + k], partner,
        )
        copy.start()
        a1_sends.append(copy)
        for t in (2, 1, 3):
            x2, y2 = (x + t) & 3, (y + t) & 3
            for n, (pos, here, target) in enumerate(
                ((x2, x, x2 * 8 + y * 2), (y2, y, x * 8 + y2 * 2 + 1))
            ):
                copy = rc(
                    mp.at[o, rows(n * half + pos * quarter, quarter, quarter), :],
                    a1[o].at[here * 2 + k], a1_send.at[o, 2 * t + n - 1],
                    a1_recv.at[o, here * 2 + k], {"pcol": target},
                )
                copy.start()
                a1_sends.append(copy)

    def finish_a1(o):
        def take(j):
            return rc(a1[o].at[j], a1[o].at[j], a1_send.at[o, 0], a1_recv.at[o, j], partner)

        pltpu.make_async_copy(a1[o].at[f * 2 + k], a1[o].at[f * 2 + k], a1_recv.at[o, f * 2 + k]).wait()
        take(f * 2 + 1 - k).wait_recv()
        for t in (1, 3, 2):
            for kk in (0, 1):
                take(((f + t) & 3) * 2 + kk).wait_recv()
        for ci in (0, 1):
            c = piv[ci, 2]
            place = jnp.where(k == 0, c >> 3, (c >> 1) & 3) * 2 + (c & 1)
            q[o][ci] = a1[o][place]

    a2_sends = []

    def start_a2(o):
        a2[o][g] = q[o][:, rows(g * PIECE, PIECE, PIECE), :]
        for t in (2, 1, 3):
            g2 = (g + t) & 3
            copy = rc(
                q[o].at[:, rows(g2 * PIECE, PIECE, PIECE), :], a2[o].at[g],
                a2_send.at[o, t - 1], a2_recv.at[o, g], dev(f, g2),
            )
            copy.start()
            a2_sends.append(copy)

    def finish_a2(o):
        for t in (1, 3, 2):
            j = (g + t) & 3
            rc(a2[o].at[j], a2[o].at[j], a2_send.at[o, 0], a2_recv.at[o, j], partner).wait_recv()
        for ci in (0, 1):
            c = piv[ci, 2]
            place = jnp.where(k == 0, (c >> 1) & 3, c >> 3)
            s_[o][ci] = a2[o][place, ci]

    base = k * half + f * quarter

    def dst(u, where):
        if u == 3:
            return xn.at[:, where, :]
        return pn.at[:, u, where, :]

    def piece(u):
        return (w, s_[1], s_[2], lp)[u]

    def spot(ff, gg):
        return rows(k * half + ff * quarter + gg * PIECE, PIECE, PIECE)

    g_sends = []

    def start_g1(u, note=True):
        pltpu.make_async_copy(piece(u), dst(u, spot(f, g)), g1_loc.at[u]).start()
        for t in (2, 1, 3):
            copy = rc(
                piece(u), dst(u, spot(f, g)), g1_send.at[u, t - 1], g1_recv.at[u, g], dev(f, (g + t) & 3)
            )
            copy.start()
            if note:
                g_sends.append(copy)

    def start_g2(u, note=True):
        pltpu.make_async_copy(piece(u), dst(u, spot(f, g)), g1_loc.at[u]).wait()
        for t in (1, 3, 2):
            j = (g + t) & 3
            rc(piece(u), dst(u, spot(f, j)), g1_send.at[u, 0], g1_recv.at[u, j], partner).wait_recv()
        block = dst(u, rows(base, quarter, quarter))
        for t in (2, 1, 3):
            copy = rc(block, block, g2_send.at[u, t - 1], g2_recv.at[u, f], dev((f + t) & 3, g))
            copy.start()
            if note:
                g_sends.append(copy)

    def start_d(u):
        for t in (1, 3, 2):
            j = (f + t) & 3
            block = dst(u, rows(k * half + j * quarter, quarter, quarter))
            rc(block, block, g2_send.at[u, 0], g2_recv.at[u, j], partner).wait_recv()
        block = dst(u, rows(k * half, half, half))
        copy = rc(block, block, d_send.at[u], d_recv.at[u], partner)
        copy.start()
        g_sends.append(copy)

    def finish_d(u):
        block = dst(u, rows((1 - k) * half, half, half))
        rc(block, block, d_send.at[u], d_recv.at[u], partner).wait_recv()

    h = jnp.where(low, z, last - z)

    def at_height(height):
        return {"prow": jnp.where(low, height, last - height) & last}

    other_edge = {"prow": last - z}
    relays = jnp.logical_and(h >= 2, h <= mid - 2)
    sinks = jnp.logical_and(h >= 2, h <= hub)
    rises = jnp.logical_and(h >= hub, h <= mid - 2)

    def row_chunk(b, i, n, device):
        block = rr.at[b, rows(i * CHUNK, CHUNK, CHUNK), :]
        return rc(block, block, r_send.at[n, b, i], r_recv.at[b, i], device)

    def source_copies(b, i):
        return (
            row_chunk(b, i, 0, {"prow": hub}),
            row_chunk(b, i, 1, {"prow": last - hub}),
            row_chunk(b, i, 2, other_edge),
        )

    def relay_step(i, carry):
        for b in (0, 1):
            fall, rise = row_chunk(b, i, 0, at_height(h - 1)), row_chunk(b, i, 1, at_height(h + 1))
            fall.wait_recv()

            @pl.when(sinks)
            def _():
                fall.start()

            @pl.when(rises)
            def _():
                rise.start()

        return carry

    def chain(lo, hi):
        lax.fori_loop(lo, hi, relay_step, 0)

    def corner(b, t):
        return rc(lp.at[b], lp.at[b], l_send.at[t - 1], l_recv.at[b], {"prow": (z + t) & last})

    for o in (0, 1, 2):
        start_a1(o)

    for b, at in ((0, 0), (1, last)):

        @pl.when(z == at)
        def _():
            copy = pltpu.make_async_copy(mp.at[0], rr.at[b], r_loc)
            copy.start()
            copy.wait()

            def send(i, carry):
                for copy in source_copies(b, i):
                    copy.start()
                return carry

            lax.fori_loop(0, FIRST, send, 0)

    receiver = {"prow": jnp.where(z == mid, 0, last)}
    sw_copy = rc(mp.at[0], sw, sw_send, sw_recv, receiver)
    w_copy = rc(s_[0], w, w_send, w_recv, receiver)

    def pass_in():
        @pl.when(jnp.logical_and(h >= 1, h < mid - 1))
        def _():
            pl.semaphore_wait(tok_in, 1)

        @pl.when(h >= 1)
        def _():
            pl.semaphore_signal(tok_in, inc=1, device_id=at_height(h - 1), device_id_type=MESH)

    def pass_out():
        @pl.when(h >= 1)
        def _():
            pl.semaphore_wait(tok_out, 1)

        @pl.when(h < mid - 1)
        def _():
            pl.semaphore_signal(tok_out, inc=1, device_id=at_height(h + 1), device_id_type=MESH)

    @pl.when(h < hub)
    def _():
        pass_out()
        pass_in()

    @pl.when(h >= hub)
    def _():
        pass_in()
        pass_out()

    @pl.when(give)
    def _():
        pl.semaphore_signal(tok_go, inc=1, device_id=other_edge, device_id_type=MESH)
        pl.semaphore_wait(tok_go, 1)
        sw_copy.start()

    begin = 130 + 33 * jnp.abs(h - hub)

    def mark(us):
        return jnp.where(relays, jnp.clip(jnp.maximum(us * 10 - begin, 0) // 12, 0, n_chunk), 0)

    marks = [mark(us) for us in (9, 12, 14, 18, 20, 22, 25, 27, 29, 33)]
    done = [0]

    def relay_to(n):
        chain(done[-1], marks[n])
        done.append(marks[n])

    relay_to(0)

    finish_a1(0)
    start_a2(0)

    relay_to(1)
    finish_a1(1)
    start_a2(1)
    finish_a2(0)

    @pl.when(edge)
    def _():
        which = jnp.where(jnp.logical_xor(z == 0, first_one), 0, 1)
        lp[jnp.where(z == 0, 0, 1)] = s_[0][which]
        pl.semaphore_wait(tok_in, 1)
        pl.semaphore_signal(tok_over, inc=1, device_id=other_edge, device_id_type=MESH)
        pl.semaphore_wait(tok_over, 1)

    @pl.when(give)
    def _():
        w_copy.start()

    for b, at in ((0, 0), (1, last)):

        @pl.when(z == at)
        def _():
            for t in (8, 7, 9, 6, 10, 5, 11, 4, 12, 3, 13, 2, 14, 1, 15):
                corner(b, t).start()

            def send(i, carry):
                for copy in source_copies(b, i):
                    copy.start()
                return carry

            lax.fori_loop(FIRST, n_chunk, send, 0)

    @pl.when(jnp.logical_not(edge))
    def _():
        w[...] = s_[0][...]
        start_g1(0, False)

    relay_to(2)
    finish_a1(2)
    start_a2(2)
    finish_a2(1)
    start_g1(1)
    relay_to(3)
    finish_a2(2)

    start_g1(2)
    relay_to(4)
    @pl.when(jnp.logical_not(edge))
    def _():
        start_g2(0, False)

    start_g2(1)
    relay_to(5)
    for b, at in ((0, 0), (1, last)):

        @pl.when(z != at)
        def _():
            corner(b, 1).wait_recv()

    start_g1(3)
    start_g2(2)
    relay_to(6)
    start_d(1)
    relay_to(7)

    @pl.when(edge)
    def _():
        w_copy.wait_recv()
        start_g1(0, False)

    start_g2(3)
    relay_to(8)
    start_d(2)

    @pl.when(edge)
    def _():
        start_g2(0, False)

    relay_to(9)
    start_d(3)
    chain(done[-1], jnp.where(relays, n_chunk, 0))
    start_d(0)
    for u in (1, 2, 3, 0):
        finish_d(u)

    @pl.when(edge)
    def _():
        sw_copy.wait_recv()

    def leaf(i, carry):
        for b, at in ((0, 0), (1, last)):

            @pl.when(z != at)
            def _():
                row_chunk(b, i, 0, other_edge).wait_recv()

        return carry

    lax.fori_loop(0, jnp.where(relays, 0, n_chunk), leaf, 0)

    @pl.when(give)
    def _():
        sw_copy.wait_send()
        w_copy.wait_send()

    for copy in a1_sends + a2_sends + g_sends:
        copy.wait_send()
    for t in (1, 2, 3):
        rc(w, w, g1_send.at[0, t - 1], g1_recv.at[0, g], partner).wait_send()
        block = dst(0, rows(base, quarter, quarter))
        rc(block, block, g2_send.at[0, t - 1], g2_recv.at[0, f], partner).wait_send()

    for b, at in ((0, 0), (1, last)):

        @pl.when(z == at)
        def _():
            for t in range(1, 16):
                corner(b, t).wait_send()

            def sent(i, carry):
                for copy in source_copies(b, i):
                    copy.wait_send()
                return carry

            lax.fori_loop(0, n_chunk, sent, 0)

    def relayed(i, carry):
        for b in (0, 1):

            @pl.when(sinks)
            def _():
                row_chunk(b, i, 0, other_edge).wait_send()

            @pl.when(rises)
            def _():
                row_chunk(b, i, 1, other_edge).wait_send()

        return carry

    lax.fori_loop(0, jnp.where(relays, n_chunk, 0), relayed, 0)


def run_gather(pivots, blocks):
    slots, size, width = blocks.shape
    n_chunk = size // CHUNK
    quarter = size // 8
    vm = pltpu.VMEM
    dma = pltpu.SemaphoreType.DMA
    scratch = (
        [vm((8, quarter, width), BF)] * 3
        + [vm((2, quarter, width), BF)] * 3
        + [vm((4, 2, PIECE, width), BF)] * 3
        + [vm((2, PIECE, width), BF)] * 5
        + [vm((slots, size, width), BF)]
        + [dma((3, 8)), dma((3, 8)), dma((3, 3)), dma((3, 4)), dma((4, 3)), dma((4, 4)), dma((4,))]
        + [dma((4, 3)), dma((4, 4)), dma((4,)), dma((4,))]
        + [dma((3, 2, n_chunk)), dma((2, n_chunk)), dma(())]
        + [dma((15,)), dma((2,))]
        + [dma(())] * 4
        + [pltpu.SemaphoreType.REGULAR] * 4
    )
    return pl.pallas_call(
        gather,
        out_shape=[
            jax.ShapeDtypeStruct((2, slots, size, width), BF),
            jax.ShapeDtypeStruct((2, size, width), BF),
            jax.ShapeDtypeStruct((2, size, width), BF),
            jax.ShapeDtypeStruct((size, width), BF),
        ],
        in_specs=[pl.BlockSpec(memory_space=pltpu.SMEM), pl.BlockSpec(memory_space=pltpu.VMEM)],
        out_specs=[pl.BlockSpec(memory_space=pltpu.VMEM)] * 4,
        scratch_shapes=scratch,
        compiler_params=pltpu.CompilerParams(collective_id=0, has_side_effects=True),
        name="gather",
    )(pivots, blocks)


def update(piv, pat, blocks, panels, corners, tops, swapped, inv, out, lead, upper):
    slots, size, width = blocks.shape
    row = lax.axis_index("prow")
    col = lax.axis_index("pcol")
    nrow = lax.axis_size("prow")
    a1, b1, c1 = piv[0, 0], piv[0, 1], piv[0, 2]
    a2, b2, c2 = piv[1, 0], piv[1, 1], piv[1, 2]
    one = jnp.where(b1 == 0, 0, 1)
    two = 1 - one

    def keep(i, j):
        return pat[i, j].astype(F32)

    def dot(left, right):
        return jnp.dot(left, right, preferred_element_type=F32)

    own1 = keep(b1, col)
    cross12 = keep(b1, c2)
    lead[...] = (dot(corners[two], inv[0]) * keep(b2, c1)).astype(BF)

    @pl.when(col == c1)
    def _():
        upper[...] = lead[...]

    @pl.when(col != c1)
    def _():
        old = tops[two].astype(F32) * keep(b2, col)
        upper[...] = (old - dot(lead[...], tops[one]) * own1).astype(BF)

    def slot(s, carry):
        here = s * nrow + row
        held = jnp.where(here == b1, a1, jnp.where(here == b2, a2, here))
        turned = s - jnp.where(row == nrow // 2, jnp.where(b1 == 0, a1, a2), jnp.where(b1 == 0, a2, a1)) // nrow
        turned = jnp.where(turned < 0, turned + slots, turned)
        give = jnp.logical_or(row == nrow // 2, row == nrow // 2 - 1)
        unit = jnp.where(give, turned, jnp.where(row < nrow // 2, s, slots - 1 - s))
        old = jnp.where(here == held, blocks[s], swapped[...]).astype(F32) * keep(held, col)
        left1 = (dot(panels[0, unit], inv[0]) * keep(held, c1)).astype(BF)
        step1 = (old - dot(left1, tops[one]) * own1).astype(BF)
        column2 = panels[1, unit].astype(F32) * keep(held, c2) - dot(left1, corners[one]) * cross12
        left2 = dot(column2.astype(BF), inv[1]).astype(BF)
        out[s] = (step1.astype(F32) - dot(left2, upper[...])).astype(BF)

        @pl.when(col == c1)
        def _():
            out[s] = left1

        @pl.when(col == c2)
        def _():
            out[s] = left2

        @pl.when(here == a1)
        def _():
            out[s] = (tops[one].astype(F32) * own1).astype(BF)

        @pl.when(here == a2)
        def _():
            out[s] = upper[...]

        return carry

    lax.fori_loop(0, slots, slot, 0)


def run_update(pivots, pattern, blocks, panels, corners, tops, swapped, inverses):
    slots, size, width = blocks.shape
    smem, vmem = pl.BlockSpec(memory_space=pltpu.SMEM), pl.BlockSpec(memory_space=pltpu.VMEM)
    return pl.pallas_call(
        update,
        out_shape=jax.ShapeDtypeStruct(blocks.shape, BF),
        in_specs=[smem, smem] + [vmem] * 6,
        out_specs=vmem,
        scratch_shapes=[pltpu.VMEM((size, width), BF)] * 2,
        name="update",
    )(pivots, pattern, blocks, panels, corners, tops, swapped, inverses)


def local(matrix, pattern, inverses, pivots):
    slots, size, _, width = matrix.shape
    blocks = matrix.reshape(slots, size, width)
    moved = run_gather(pivots, blocks)
    return run_update(pivots, pattern, blocks, *moved, inverses).reshape(matrix.shape)


def solution(mesh):
    placed = (P(None, "prow", None, "pcol"), P(), P(), P())
    return jax.shard_map(
        local, mesh=mesh, in_specs=placed, out_specs=P(None, "prow", None, "pcol"), check_vma=False
    )
```

```python
import jax
import jax.numpy as jnp
from jax import lax
from jax.experimental import pallas as pl
from jax.experimental.pallas import tpu as pltpu
from jax.sharding import PartitionSpec as P

BF = jnp.bfloat16
F32 = jnp.float32
MESH = pl.DeviceIdType.MESH
PIECE = 16
CHUNK = 32
FIRST = 8


def gather(piv, m, pn, xn, rr, sw, *scratch):
    (a1_0, a1_1, a1_2, q_0, q_1, q_2, a2_0, a2_1, a2_2, s_0, s_1, s_2, lp, w, mp,
     a1_send, a1_recv, a2_send, a2_recv, g1_send, g1_recv, g1_loc, g2_send, g2_recv,
     d_send, d_recv, r_send, r_recv, r_loc, l_send, l_recv,
     sw_send, sw_recv, w_send, w_recv, tok_in, tok_over) = scratch
    a1, q, a2, s_ = (a1_0, a1_1, a1_2), (q_0, q_1, q_2), (a2_0, a2_1, a2_2), (s_0, s_1, s_2)
    size = m.shape[1]
    half, quarter = size // 2, size // 8
    n_chunk = size // CHUNK
    z = lax.axis_index("prow")
    p = lax.axis_index("pcol")
    nz = lax.axis_size("prow")
    mid = nz // 2
    last = nz - 1
    x, y, k = p >> 3, (p >> 1) & 3, p & 1
    f, g = jnp.where(k == 0, x, y), jnp.where(k == 0, y, x)
    low = z < mid
    edge = jnp.logical_or(z == 0, z == last)
    first_one = piv[0, 1] == 0

    def dev(ff, gg):
        xx, yy = jnp.where(k == 0, ff, gg), jnp.where(k == 0, gg, ff)
        return {"pcol": xx * 8 + yy * 2 + k}

    partner = {"pcol": p ^ 1}

    def rc(src, dst, send, recv, device):
        return pltpu.make_async_remote_copy(
            src_ref=src, dst_ref=dst, send_sem=send, recv_sem=recv, device_id=device, device_id_type=MESH
        )

    def rows(start, count, align):
        return pl.ds(pl.multiple_of(start, align), count)

    barrier = pltpu.get_barrier_semaphore()
    mates = [partner]
    for t in (1, 2, 3):
        for kk in (0, 1):
            mates.append({"pcol": ((x + t) & 3) * 8 + y * 2 + kk})
            mates.append({"pcol": x * 8 + ((y + t) & 3) * 2 + kk})
    mates.append({"prow": (z + 1) & last})
    mates.append({"prow": (z + last) & last})
    for mate in mates:
        pl.semaphore_signal(barrier, inc=1, device_id=mate, device_id_type=MESH)
    hub = mid // 2 - 1

    @pl.when(jnp.logical_or(z == hub, z == last - hub))
    def _():
        for at in (0, last):
            pl.semaphore_signal(barrier, inc=1, device_id={"prow": at}, device_id_type=MESH)

    give = jnp.logical_or(z == mid, z == mid - 1)

    @pl.when(edge)
    def _():
        pl.semaphore_signal(barrier, inc=1, device_id={"prow": z ^ mid}, device_id_type=MESH)

    extra = jnp.where(edge, 2, jnp.where(give, 1, 0))
    pl.semaphore_wait(barrier, len(mates) + extra)

    slot_a = jnp.where(jnp.logical_xor(z == mid, first_one), piv[1, 0], piv[0, 0]) >> 4
    for u in (0, 1, 2):
        turned = slot_a + u
        mp[u] = m[jnp.where(give, jnp.where(turned > 2, turned - 3, turned), jnp.where(low, u, 2 - u))]

    a1_sends = []

    def start_a1(o):
        own = pltpu.make_async_copy(
            mp.at[o, rows(k * half + f * quarter, quarter, quarter), :],
            a1[o].at[f * 2 + k], a1_recv.at[o, f * 2 + k],
        )
        own.start()
        copy = rc(
            mp.at[o, rows((1 - k) * half + g * quarter, quarter, quarter), :],
            a1[o].at[g * 2 + k], a1_send.at[o, 0], a1_recv.at[o, g * 2 + k], partner,
        )
        copy.start()
        a1_sends.append(copy)
        for t in (2, 1, 3):
            x2, y2 = (x + t) & 3, (y + t) & 3
            for n, (pos, here, target) in enumerate(
                ((x2, x, x2 * 8 + y * 2), (y2, y, x * 8 + y2 * 2 + 1))
            ):
                copy = rc(
                    mp.at[o, rows(n * half + pos * quarter, quarter, quarter), :],
                    a1[o].at[here * 2 + k], a1_send.at[o, 2 * t + n - 1],
                    a1_recv.at[o, here * 2 + k], {"pcol": target},
                )
                copy.start()
                a1_sends.append(copy)

    def finish_a1(o):
        def take(j):
            return rc(a1[o].at[j], a1[o].at[j], a1_send.at[o, 0], a1_recv.at[o, j], partner)

        pltpu.make_async_copy(a1[o].at[f * 2 + k], a1[o].at[f * 2 + k], a1_recv.at[o, f * 2 + k]).wait()
        take(f * 2 + 1 - k).wait_recv()
        for t in (1, 3, 2):
            for kk in (0, 1):
                take(((f + t) & 3) * 2 + kk).wait_recv()
        for ci in (0, 1):
            c = piv[ci, 2]
            place = jnp.where(k == 0, c >> 3, (c >> 1) & 3) * 2 + (c & 1)
            q[o][ci] = a1[o][place]

    a2_sends = []

    def start_a2(o):
        a2[o][g] = q[o][:, rows(g * PIECE, PIECE, PIECE), :]
        for t in (2, 1, 3):
            g2 = (g + t) & 3
            copy = rc(
                q[o].at[:, rows(g2 * PIECE, PIECE, PIECE), :], a2[o].at[g],
                a2_send.at[o, t - 1], a2_recv.at[o, g], dev(f, g2),
            )
            copy.start()
            a2_sends.append(copy)

    def finish_a2(o):
        for t in (1, 3, 2):
            j = (g + t) & 3
            rc(a2[o].at[j], a2[o].at[j], a2_send.at[o, 0], a2_recv.at[o, j], partner).wait_recv()
        for ci in (0, 1):
            c = piv[ci, 2]
            place = jnp.where(k == 0, (c >> 1) & 3, c >> 3)
            s_[o][ci] = a2[o][place, ci]

    base = k * half + f * quarter

    def dst(u, where):
        if u == 3:
            return xn.at[:, where, :]
        return pn.at[:, u, where, :]

    def piece(u):
        return (w, s_[1], s_[2], lp)[u]

    def spot(ff, gg):
        return rows(k * half + ff * quarter + gg * PIECE, PIECE, PIECE)

    g_sends = []

    def start_g1(u, note=True):
        pltpu.make_async_copy(piece(u), dst(u, spot(f, g)), g1_loc.at[u]).start()
        for t in (2, 1, 3):
            copy = rc(
                piece(u), dst(u, spot(f, g)), g1_send.at[u, t - 1], g1_recv.at[u, g], dev(f, (g + t) & 3)
            )
            copy.start()
            if note:
                g_sends.append(copy)

    def start_g2(u, note=True):
        pltpu.make_async_copy(piece(u), dst(u, spot(f, g)), g1_loc.at[u]).wait()
        for t in (1, 3, 2):
            j = (g + t) & 3
            rc(piece(u), dst(u, spot(f, j)), g1_send.at[u, 0], g1_recv.at[u, j], partner).wait_recv()
        block = dst(u, rows(base, quarter, quarter))
        for t in (2, 1, 3):
            copy = rc(block, block, g2_send.at[u, t - 1], g2_recv.at[u, f], dev((f + t) & 3, g))
            copy.start()
            if note:
                g_sends.append(copy)

    def start_d(u):
        for t in (1, 3, 2):
            j = (f + t) & 3
            block = dst(u, rows(k * half + j * quarter, quarter, quarter))
            rc(block, block, g2_send.at[u, 0], g2_recv.at[u, j], partner).wait_recv()
        block = dst(u, rows(k * half, half, half))
        copy = rc(block, block, d_send.at[u], d_recv.at[u], partner)
        copy.start()
        g_sends.append(copy)

    def finish_d(u):
        block = dst(u, rows((1 - k) * half, half, half))
        rc(block, block, d_send.at[u], d_recv.at[u], partner).wait_recv()

    h = jnp.where(low, z, last - z)

    def at_height(height):
        return {"prow": jnp.where(low, height, last - height) & last}

    other_edge = {"prow": last - z}
    relays = jnp.logical_and(h >= 2, h <= mid - 2)
    sinks = jnp.logical_and(h >= 2, h <= hub)
    rises = jnp.logical_and(h >= hub, h <= mid - 2)

    def row_chunk(b, i, n, device):
        block = rr.at[b, rows(i * CHUNK, CHUNK, CHUNK), :]
        return rc(block, block, r_send.at[n, b, i], r_recv.at[b, i], device)

    def source_copies(b, i):
        return (
            row_chunk(b, i, 0, {"prow": hub}),
            row_chunk(b, i, 1, {"prow": last - hub}),
            row_chunk(b, i, 2, other_edge),
        )

    def relay_step(i, carry):
        for b in (0, 1):
            fall, rise = row_chunk(b, i, 0, at_height(h - 1)), row_chunk(b, i, 1, at_height(h + 1))
            fall.wait_recv()

            @pl.when(sinks)
            def _():
                fall.start()

            @pl.when(rises)
            def _():
                rise.start()

        return carry

    def chain(lo, hi):
        lax.fori_loop(lo, hi, relay_step, 0)

    def corner(b, t):
        return rc(lp.at[b], lp.at[b], l_send.at[t - 1], l_recv.at[b], {"prow": (z + t) & last})

    for o in (0, 1, 2):
        start_a1(o)
    receiver = {"prow": jnp.where(z == mid, 0, last)}
    sw_copy = rc(mp.at[0], sw, sw_send, sw_recv, receiver)

    @pl.when(give)
    def _():
        sw_copy.start()


    for b, at in ((0, 0), (1, last)):

        @pl.when(z == at)
        def _():
            copy = pltpu.make_async_copy(mp.at[0], rr.at[b], r_loc)
            copy.start()
            copy.wait()

            def send(i, carry):
                for copy in source_copies(b, i):
                    copy.start()
                return carry

            lax.fori_loop(0, FIRST, send, 0)

    w_copy = rc(s_[0], w, w_send, w_recv, receiver)

    def pass_in():
        @pl.when(jnp.logical_and(h >= 1, h < mid - 1))
        def _():
            pl.semaphore_wait(tok_in, 1)

        @pl.when(h >= 1)
        def _():
            pl.semaphore_signal(tok_in, inc=1, device_id=at_height(h - 1), device_id_type=MESH)

    pass_in()

    begin = 130 + 33 * jnp.abs(h - hub)

    def mark(us):
        return jnp.where(relays, jnp.clip(jnp.maximum(us * 10 - begin, 0) // 12, 0, n_chunk), 0)

    marks = [mark(us) for us in (9, 12, 14, 18, 20, 22, 25, 27, 29, 33)]
    done = [0]

    def relay_to(n):
        chain(done[-1], marks[n])
        done.append(marks[n])

    relay_to(0)

    finish_a1(0)
    start_a2(0)

    relay_to(1)
    finish_a1(1)
    start_a2(1)
    finish_a2(0)

    @pl.when(edge)
    def _():
        which = jnp.where(jnp.logical_xor(z == 0, first_one), 0, 1)
        lp[jnp.where(z == 0, 0, 1)] = s_[0][which]
        pl.semaphore_wait(tok_in, 1)
        pl.semaphore_signal(tok_over, inc=1, device_id=other_edge, device_id_type=MESH)
        pl.semaphore_wait(tok_over, 1)

    @pl.when(give)
    def _():
        w_copy.start()

    for b, at in ((0, 0), (1, last)):

        @pl.when(z == at)
        def _():
            for t in (8, 7, 9, 6, 10, 5, 11, 4, 12, 3, 13, 2, 14, 1, 15):
                corner(b, t).start()

            def send(i, carry):
                for copy in source_copies(b, i):
                    copy.start()
                return carry

            lax.fori_loop(FIRST, n_chunk, send, 0)

    @pl.when(jnp.logical_not(edge))
    def _():
        w[...] = s_[0][...]
        start_g1(0, False)

    relay_to(2)
    finish_a1(2)
    start_a2(2)
    finish_a2(1)
    start_g1(1)
    relay_to(3)
    finish_a2(2)

    start_g1(2)
    relay_to(4)
    @pl.when(jnp.logical_not(edge))
    def _():
        start_g2(0, False)

    start_g2(1)
    relay_to(5)
    for b, at in ((0, 0), (1, last)):

        @pl.when(z != at)
        def _():
            corner(b, 1).wait_recv()

    start_g1(3)
    start_g2(2)
    relay_to(6)
    start_d(1)
    relay_to(7)

    @pl.when(edge)
    def _():
        w_copy.wait_recv()
        start_g1(0, False)

    start_g2(3)
    relay_to(8)
    start_d(2)

    @pl.when(edge)
    def _():
        start_g2(0, False)

    relay_to(9)
    start_d(3)
    chain(done[-1], jnp.where(relays, n_chunk, 0))
    start_d(0)
    for u in (1, 2, 3, 0):
        finish_d(u)

    @pl.when(edge)
    def _():
        sw_copy.wait_recv()

    def leaf(i, carry):
        for b, at in ((0, 0), (1, last)):

            @pl.when(z != at)
            def _():
                row_chunk(b, i, 0, other_edge).wait_recv()

        return carry

    lax.fori_loop(0, jnp.where(relays, 0, n_chunk), leaf, 0)

    @pl.when(give)
    def _():
        sw_copy.wait_send()
        w_copy.wait_send()

    for copy in a1_sends + a2_sends + g_sends:
        copy.wait_send()
    for t in (1, 2, 3):
        rc(w, w, g1_send.at[0, t - 1], g1_recv.at[0, g], partner).wait_send()
        block = dst(0, rows(base, quarter, quarter))
        rc(block, block, g2_send.at[0, t - 1], g2_recv.at[0, f], partner).wait_send()

    for b, at in ((0, 0), (1, last)):

        @pl.when(z == at)
        def _():
            for t in range(1, 16):
                corner(b, t).wait_send()

            def sent(i, carry):
                for copy in source_copies(b, i):
                    copy.wait_send()
                return carry

            lax.fori_loop(0, n_chunk, sent, 0)

    def relayed(i, carry):
        for b in (0, 1):

            @pl.when(sinks)
            def _():
                row_chunk(b, i, 0, other_edge).wait_send()

            @pl.when(rises)
            def _():
                row_chunk(b, i, 1, other_edge).wait_send()

        return carry

    lax.fori_loop(0, jnp.where(relays, n_chunk, 0), relayed, 0)


def run_gather(pivots, blocks):
    slots, size, width = blocks.shape
    n_chunk = size // CHUNK
    quarter = size // 8
    vm = pltpu.VMEM
    dma = pltpu.SemaphoreType.DMA
    scratch = (
        [vm((8, quarter, width), BF)] * 3
        + [vm((2, quarter, width), BF)] * 3
        + [vm((4, 2, PIECE, width), BF)] * 3
        + [vm((2, PIECE, width), BF)] * 5
        + [vm((slots, size, width), BF)]
        + [dma((3, 8)), dma((3, 8)), dma((3, 3)), dma((3, 4)), dma((4, 3)), dma((4, 4)), dma((4,))]
        + [dma((4, 3)), dma((4, 4)), dma((4,)), dma((4,))]
        + [dma((3, 2, n_chunk)), dma((2, n_chunk)), dma(())]
        + [dma((15,)), dma((2,))]
        + [dma(())] * 4
        + [pltpu.SemaphoreType.REGULAR] * 2
    )
    return pl.pallas_call(
        gather,
        out_shape=[
            jax.ShapeDtypeStruct((2, slots, size, width), BF),
            jax.ShapeDtypeStruct((2, size, width), BF),
            jax.ShapeDtypeStruct((2, size, width), BF),
            jax.ShapeDtypeStruct((size, width), BF),
        ],
        in_specs=[pl.BlockSpec(memory_space=pltpu.SMEM), pl.BlockSpec(memory_space=pltpu.VMEM)],
        out_specs=[pl.BlockSpec(memory_space=pl.ANY)] * 4,
        scratch_shapes=scratch,
        compiler_params=pltpu.CompilerParams(collective_id=0, has_side_effects=True),
        name="gather",
    )(pivots, blocks)


def update(piv, pat, blocks, panels, corners, tops, swapped, inv, out, lead, upper):
    slots, size, width = blocks.shape
    row = lax.axis_index("prow")
    col = lax.axis_index("pcol")
    nrow = lax.axis_size("prow")
    a1, b1, c1 = piv[0, 0], piv[0, 1], piv[0, 2]
    a2, b2, c2 = piv[1, 0], piv[1, 1], piv[1, 2]
    one = jnp.where(b1 == 0, 0, 1)
    two = 1 - one

    def keep(i, j):
        return pat[j, i].astype(F32)

    def dot(left, right):
        return jnp.dot(left, right, preferred_element_type=F32)

    own1 = keep(b1, col)
    cross12 = keep(b1, c2)
    lead[...] = (dot(corners[two], inv[0]) * keep(b2, c1)).astype(BF)

    @pl.when(col == c1)
    def _():
        upper[...] = lead[...]

    @pl.when(col != c1)
    def _():
        old = tops[two].astype(F32) * keep(b2, col)
        upper[...] = (old - dot(lead[...], tops[one]) * own1).astype(BF)

    def slot(s, carry):
        here = s * nrow + row
        held = jnp.where(here == b1, a1, jnp.where(here == b2, a2, here))
        turned = s - jnp.where(row == nrow // 2, jnp.where(b1 == 0, a1, a2), jnp.where(b1 == 0, a2, a1)) // nrow
        turned = jnp.where(turned < 0, turned + slots, turned)
        give = jnp.logical_or(row == nrow // 2, row == nrow // 2 - 1)
        unit = jnp.where(give, turned, jnp.where(row < nrow // 2, s, slots - 1 - s))
        old = jnp.where(here == held, blocks[s], swapped[...]).astype(F32) * keep(held, col)
        left1 = (dot(panels[0, unit], inv[0]) * keep(held, c1)).astype(BF)
        step1 = (old - dot(left1, tops[one]) * own1).astype(BF)
        column2 = panels[1, unit].astype(F32) * keep(held, c2) - dot(left1, corners[one]) * cross12
        left2 = dot(column2.astype(BF), inv[1]).astype(BF)
        out[s] = (step1.astype(F32) - dot(left2, upper[...])).astype(BF)

        @pl.when(col == c1)
        def _():
            out[s] = left1

        @pl.when(col == c2)
        def _():
            out[s] = left2

        @pl.when(here == a1)
        def _():
            out[s] = (tops[one].astype(F32) * own1).astype(BF)

        @pl.when(here == a2)
        def _():
            out[s] = upper[...]

        return carry

    lax.fori_loop(0, slots, slot, 0)


def run_update(pivots, pattern, blocks, panels, corners, tops, swapped, inverses):
    slots, size, width = blocks.shape
    smem, vmem = pl.BlockSpec(memory_space=pltpu.SMEM), pl.BlockSpec(memory_space=pltpu.VMEM)
    return pl.pallas_call(
        update,
        out_shape=jax.ShapeDtypeStruct(blocks.shape, BF),
        in_specs=[smem, smem] + [vmem] * 6,
        out_specs=vmem,
        scratch_shapes=[pltpu.VMEM((size, width), BF)] * 2,
        name="update",
    )(pivots, pattern, blocks, panels, corners, tops, swapped, inverses)


def local(matrix, pattern, inverses, pivots):
    slots, size, _, width = matrix.shape
    blocks = matrix.reshape(slots, size, width)
    moved = run_gather(pivots, blocks)
    return run_update(pivots, pattern.T, blocks, *moved, inverses).reshape(matrix.shape)


def solution(mesh):
    placed = (P(None, "prow", None, "pcol"), P(), P(), P())
    return jax.shard_map(
        local, mesh=mesh, in_specs=placed, out_specs=P(None, "prow", None, "pcol"), check_vma=False
    )
```

```python
import jax
import jax.numpy as jnp
from jax import lax
from jax.experimental import pallas as pl
from jax.experimental.pallas import tpu as pltpu
from jax.sharding import PartitionSpec as P

BF = jnp.bfloat16
F32 = jnp.float32
MESH = pl.DeviceIdType.MESH
PIECE = 16
CHUNK = 32
FIRST = 8


def gather(piv, m, pn, xn, rr, sw, *scratch):
    (a1_0, a1_1, a1_2, q_0, q_1, q_2, a2_0, a2_1, a2_2, s_0, s_1, s_2, lp, w, mp,
     a1_send, a1_recv, a2_send, a2_recv, g1_send, g1_recv, g1_loc, g2_send, g2_recv,
     d_send, d_recv, r_send, r_recv, r_loc, l_send, l_recv,
     sw_send, sw_recv, w_send, w_recv, tok_in, tok_over) = scratch
    a1, q, a2, s_ = (a1_0, a1_1, a1_2), (q_0, q_1, q_2), (a2_0, a2_1, a2_2), (s_0, s_1, s_2)
    size = m.shape[1]
    half, quarter = size // 2, size // 8
    n_chunk = size // CHUNK
    z = lax.axis_index("prow")
    p = lax.axis_index("pcol")
    nz = lax.axis_size("prow")
    mid = nz // 2
    last = nz - 1
    x, y, k = p >> 3, (p >> 1) & 3, p & 1
    f, g = jnp.where(k == 0, x, y), jnp.where(k == 0, y, x)
    low = z < mid
    edge = jnp.logical_or(z == 0, z == last)
    first_one = piv[0, 1] == 0

    def dev(ff, gg):
        xx, yy = jnp.where(k == 0, ff, gg), jnp.where(k == 0, gg, ff)
        return {"pcol": xx * 8 + yy * 2 + k}

    partner = {"pcol": p ^ 1}

    def rc(src, dst, send, recv, device):
        return pltpu.make_async_remote_copy(
            src_ref=src, dst_ref=dst, send_sem=send, recv_sem=recv, device_id=device, device_id_type=MESH
        )

    def rows(start, count, align):
        return pl.ds(pl.multiple_of(start, align), count)

    barrier = pltpu.get_barrier_semaphore()
    mates = [partner]
    for t in (1, 2, 3):
        for kk in (0, 1):
            mates.append({"pcol": ((x + t) & 3) * 8 + y * 2 + kk})
            mates.append({"pcol": x * 8 + ((y + t) & 3) * 2 + kk})
    mates.append({"prow": (z + 1) & last})
    mates.append({"prow": (z + last) & last})
    for mate in mates:
        pl.semaphore_signal(barrier, inc=1, device_id=mate, device_id_type=MESH)
    hub = mid // 2 - 1

    @pl.when(jnp.logical_or(z == hub, z == last - hub))
    def _():
        for at in (0, last):
            pl.semaphore_signal(barrier, inc=1, device_id={"prow": at}, device_id_type=MESH)

    give = jnp.logical_or(z == mid, z == mid - 1)

    @pl.when(edge)
    def _():
        pl.semaphore_signal(barrier, inc=1, device_id={"prow": z ^ mid}, device_id_type=MESH)

    extra = jnp.where(edge, 2, jnp.where(give, 1, 0))
    pl.semaphore_wait(barrier, len(mates) + extra)

    slot_a = jnp.where(jnp.logical_xor(z == mid, first_one), piv[1, 0], piv[0, 0]) >> 4
    for u in (0, 1, 2):
        turned = slot_a + u
        mp[u] = m[jnp.where(give, jnp.where(turned > 2, turned - 3, turned), jnp.where(low, u, 2 - u))]

    a1_sends = []

    def start_a1(o):
        own = pltpu.make_async_copy(
            mp.at[o, rows(k * half + f * quarter, quarter, quarter), :],
            a1[o].at[f * 2 + k], a1_recv.at[o, f * 2 + k],
        )
        own.start()
        copy = rc(
            mp.at[o, rows((1 - k) * half + g * quarter, quarter, quarter), :],
            a1[o].at[g * 2 + k], a1_send.at[o, 0], a1_recv.at[o, g * 2 + k], partner,
        )
        copy.start()
        a1_sends.append(copy)
        for t in (2, 1, 3):
            x2, y2 = (x + t) & 3, (y + t) & 3
            for n, (pos, here, target) in enumerate(
                ((x2, x, x2 * 8 + y * 2), (y2, y, x * 8 + y2 * 2 + 1))
            ):
                copy = rc(
                    mp.at[o, rows(n * half + pos * quarter, quarter, quarter), :],
                    a1[o].at[here * 2 + k], a1_send.at[o, 2 * t + n - 1],
                    a1_recv.at[o, here * 2 + k], {"pcol": target},
                )
                copy.start()
                a1_sends.append(copy)

    def finish_a1(o):
        def take(j):
            return rc(a1[o].at[j], a1[o].at[j], a1_send.at[o, 0], a1_recv.at[o, j], partner)

        pltpu.make_async_copy(a1[o].at[f * 2 + k], a1[o].at[f * 2 + k], a1_recv.at[o, f * 2 + k]).wait()
        take(f * 2 + 1 - k).wait_recv()
        for t in (1, 3, 2):
            for kk in (0, 1):
                take(((f + t) & 3) * 2 + kk).wait_recv()
        for ci in (0, 1):
            c = piv[ci, 2]
            place = jnp.where(k == 0, c >> 3, (c >> 1) & 3) * 2 + (c & 1)
            q[o][ci] = a1[o][place]

    a2_sends = []

    def start_a2(o):
        a2[o][g] = q[o][:, rows(g * PIECE, PIECE, PIECE), :]
        for t in (2, 1, 3):
            g2 = (g + t) & 3
            copy = rc(
                q[o].at[:, rows(g2 * PIECE, PIECE, PIECE), :], a2[o].at[g],
                a2_send.at[o, t - 1], a2_recv.at[o, g], dev(f, g2),
            )
            copy.start()
            a2_sends.append(copy)

    def finish_a2(o):
        for t in (1, 3, 2):
            j = (g + t) & 3
            rc(a2[o].at[j], a2[o].at[j], a2_send.at[o, 0], a2_recv.at[o, j], partner).wait_recv()
        for ci in (0, 1):
            c = piv[ci, 2]
            place = jnp.where(k == 0, (c >> 1) & 3, c >> 3)
            s_[o][ci] = a2[o][place, ci]

    base = k * half + f * quarter

    def dst(u, where):
        if u == 3:
            return xn.at[:, where, :]
        return pn.at[:, u, where, :]

    def piece(u):
        return (w, s_[1], s_[2], lp)[u]

    def spot(ff, gg):
        return rows(k * half + ff * quarter + gg * PIECE, PIECE, PIECE)

    g_sends = []

    def start_g1(u, note=True):
        pltpu.make_async_copy(piece(u), dst(u, spot(f, g)), g1_loc.at[u]).start()
        for t in (2, 1, 3):
            copy = rc(
                piece(u), dst(u, spot(f, g)), g1_send.at[u, t - 1], g1_recv.at[u, g], dev(f, (g + t) & 3)
            )
            copy.start()
            if note:
                g_sends.append(copy)

    def start_g2(u, note=True):
        pltpu.make_async_copy(piece(u), dst(u, spot(f, g)), g1_loc.at[u]).wait()
        for t in (1, 3, 2):
            j = (g + t) & 3
            rc(piece(u), dst(u, spot(f, j)), g1_send.at[u, 0], g1_recv.at[u, j], partner).wait_recv()
        block = dst(u, rows(base, quarter, quarter))
        for t in (2, 1, 3):
            copy = rc(block, block, g2_send.at[u, t - 1], g2_recv.at[u, f], dev((f + t) & 3, g))
            copy.start()
            if note:
                g_sends.append(copy)

    def start_d(u):
        for t in (1, 3, 2):
            j = (f + t) & 3
            block = dst(u, rows(k * half + j * quarter, quarter, quarter))
            rc(block, block, g2_send.at[u, 0], g2_recv.at[u, j], partner).wait_recv()
        block = dst(u, rows(k * half, half, half))
        copy = rc(block, block, d_send.at[u], d_recv.at[u], partner)
        copy.start()
        g_sends.append(copy)

    def finish_d(u):
        block = dst(u, rows((1 - k) * half, half, half))
        rc(block, block, d_send.at[u], d_recv.at[u], partner).wait_recv()

    h = jnp.where(low, z, last - z)

    def at_height(height):
        return {"prow": jnp.where(low, height, last - height) & last}

    other_edge = {"prow": last - z}
    relays = jnp.logical_and(h >= 2, h <= mid - 2)
    sinks = jnp.logical_and(h >= 2, h <= hub)
    rises = jnp.logical_and(h >= hub, h <= mid - 2)

    def row_chunk(b, i, n, device):
        block = rr.at[b, rows(i * CHUNK, CHUNK, CHUNK), :]
        return rc(block, block, r_send.at[n, b, i], r_recv.at[b, i], device)

    def source_copies(b, i):
        return (
            row_chunk(b, i, 0, {"prow": hub}),
            row_chunk(b, i, 1, {"prow": last - hub}),
            row_chunk(b, i, 2, other_edge),
        )

    def relay_step(i, carry):
        for b in (0, 1):
            fall, rise = row_chunk(b, i, 0, at_height(h - 1)), row_chunk(b, i, 1, at_height(h + 1))
            fall.wait_recv()

            @pl.when(sinks)
            def _():
                fall.start()

            @pl.when(rises)
            def _():
                rise.start()

        return carry

    def chain(lo, hi):
        lax.fori_loop(lo, hi, relay_step, 0)

    def corner(b, t):
        return rc(lp.at[b], lp.at[b], l_send.at[t - 1], l_recv.at[b], {"prow": (z + t) & last})

    for o in (0, 1, 2):
        start_a1(o)
    receiver = {"prow": jnp.where(z == mid, 0, last)}
    sw_copy = rc(mp.at[0], sw, sw_send, sw_recv, receiver)

    @pl.when(give)
    def _():
        sw_copy.start()


    for b, at in ((0, 0), (1, last)):

        @pl.when(z == at)
        def _():
            copy = pltpu.make_async_copy(mp.at[0], rr.at[b], r_loc)
            copy.start()
            copy.wait()

            def send(i, carry):
                for copy in source_copies(b, i):
                    copy.start()
                return carry

            lax.fori_loop(0, FIRST, send, 0)

    w_copy = rc(s_[0], w, w_send, w_recv, receiver)

    def pass_in():
        @pl.when(jnp.logical_and(h >= 1, h < mid - 1))
        def _():
            pl.semaphore_wait(tok_in, 1)

        @pl.when(h >= 1)
        def _():
            pl.semaphore_signal(tok_in, inc=1, device_id=at_height(h - 1), device_id_type=MESH)

    pass_in()

    begin = 130 + 33 * jnp.abs(h - hub)

    def mark(us):
        return jnp.where(relays, jnp.clip(jnp.maximum(us * 10 - begin, 0) // 12, 0, n_chunk), 0)

    marks = [mark(us) for us in (9, 12, 14, 18, 20, 22, 25, 27, 29, 33)]
    done = [0]

    def relay_to(n):
        chain(done[-1], marks[n])
        done.append(marks[n])

    relay_to(0)

    finish_a1(0)
    start_a2(0)

    relay_to(1)
    finish_a1(1)
    start_a2(1)
    finish_a2(0)

    @pl.when(edge)
    def _():
        which = jnp.where(jnp.logical_xor(z == 0, first_one), 0, 1)
        lp[jnp.where(z == 0, 0, 1)] = s_[0][which]
        pl.semaphore_wait(tok_in, 1)
        pl.semaphore_signal(tok_over, inc=1, device_id=other_edge, device_id_type=MESH)
        pl.semaphore_wait(tok_over, 1)

    @pl.when(give)
    def _():
        w_copy.start()

    for b, at in ((0, 0), (1, last)):

        @pl.when(z == at)
        def _():
            for t in (8, 7, 9, 6, 10, 5, 11, 4, 12, 3, 13, 2, 14, 1, 15):
                corner(b, t).start()

            def send(i, carry):
                for copy in source_copies(b, i):
                    copy.start()
                return carry

            lax.fori_loop(FIRST, n_chunk, send, 0)

    @pl.when(jnp.logical_not(edge))
    def _():
        w[...] = s_[0][...]
        start_g1(0, False)

    relay_to(2)
    finish_a1(2)
    start_a2(2)
    finish_a2(1)
    start_g1(1)
    relay_to(3)
    finish_a2(2)

    start_g1(2)
    relay_to(4)
    @pl.when(jnp.logical_not(edge))
    def _():
        start_g2(0, False)

    start_g2(1)
    relay_to(5)
    for b, at in ((0, 0), (1, last)):

        @pl.when(z != at)
        def _():
            corner(b, 1).wait_recv()

    start_g1(3)
    start_g2(2)
    relay_to(6)
    start_d(1)
    relay_to(7)

    @pl.when(edge)
    def _():
        w_copy.wait_recv()
        start_g1(0, False)

    start_g2(3)
    relay_to(8)
    start_d(2)

    @pl.when(edge)
    def _():
        start_g2(0, False)

    relay_to(9)
    start_d(3)
    chain(done[-1], jnp.where(relays, n_chunk, 0))
    start_d(0)
    for u in (1, 2, 3, 0):
        finish_d(u)

    @pl.when(edge)
    def _():
        sw_copy.wait_recv()

    def leaf(i, carry):
        for b, at in ((0, 0), (1, last)):

            @pl.when(z != at)
            def _():
                row_chunk(b, i, 0, other_edge).wait_recv()

        return carry

    lax.fori_loop(0, jnp.where(relays, 0, n_chunk), leaf, 0)

    @pl.when(give)
    def _():
        sw_copy.wait_send()
        w_copy.wait_send()

    for copy in a1_sends + a2_sends + g_sends:
        copy.wait_send()
    for t in (1, 2, 3):
        rc(w, w, g1_send.at[0, t - 1], g1_recv.at[0, g], partner).wait_send()
        block = dst(0, rows(base, quarter, quarter))
        rc(block, block, g2_send.at[0, t - 1], g2_recv.at[0, f], partner).wait_send()

    for b, at in ((0, 0), (1, last)):

        @pl.when(z == at)
        def _():
            for t in range(1, 16):
                corner(b, t).wait_send()

            def sent(i, carry):
                for copy in source_copies(b, i):
                    copy.wait_send()
                return carry

            lax.fori_loop(0, n_chunk, sent, 0)

    def relayed(i, carry):
        for b in (0, 1):

            @pl.when(sinks)
            def _():
                row_chunk(b, i, 0, other_edge).wait_send()

            @pl.when(rises)
            def _():
                row_chunk(b, i, 1, other_edge).wait_send()

        return carry

    lax.fori_loop(0, jnp.where(relays, n_chunk, 0), relayed, 0)


def run_gather(pivots, blocks):
    slots, size, width = blocks.shape
    n_chunk = size // CHUNK
    quarter = size // 8
    vm = pltpu.VMEM
    dma = pltpu.SemaphoreType.DMA
    scratch = (
        [vm((8, quarter, width), BF)] * 3
        + [vm((2, quarter, width), BF)] * 3
        + [vm((4, 2, PIECE, width), BF)] * 3
        + [vm((2, PIECE, width), BF)] * 5
        + [vm((slots, size, width), BF)]
        + [dma((3, 8)), dma((3, 8)), dma((3, 3)), dma((3, 4)), dma((4, 3)), dma((4, 4)), dma((4,))]
        + [dma((4, 3)), dma((4, 4)), dma((4,)), dma((4,))]
        + [dma((3, 2, n_chunk)), dma((2, n_chunk)), dma(())]
        + [dma((15,)), dma((2,))]
        + [dma(())] * 4
        + [pltpu.SemaphoreType.REGULAR] * 2
    )
    return pl.pallas_call(
        gather,
        out_shape=[
            jax.ShapeDtypeStruct((2, slots, size, width), BF),
            jax.ShapeDtypeStruct((2, size, width), BF),
            jax.ShapeDtypeStruct((2, size, width), BF),
            jax.ShapeDtypeStruct((size, width), BF),
        ],
        in_specs=[pl.BlockSpec(memory_space=pltpu.SMEM), pl.BlockSpec(memory_space=pltpu.VMEM)],
        out_specs=[pl.BlockSpec(memory_space=pl.ANY)] * 4,
        scratch_shapes=scratch,
        compiler_params=pltpu.CompilerParams(collective_id=0, has_side_effects=True),
        name="gather",
    )(pivots, blocks)


def update(piv, pat, blocks_far, panels_far, corners, tops, swapped_far, inv, out, lead, upper, blocks, panels, swapped, sems):
    loads = [
        pltpu.make_async_copy(panels_far, panels, sems.at[0]),
        pltpu.make_async_copy(blocks_far, blocks, sems.at[1]),
        pltpu.make_async_copy(swapped_far, swapped, sems.at[2]),
    ]
    for load in loads:
        load.start()
    slots, size, width = blocks.shape
    row = lax.axis_index("prow")
    col = lax.axis_index("pcol")
    nrow = lax.axis_size("prow")
    a1, b1, c1 = piv[0, 0], piv[0, 1], piv[0, 2]
    a2, b2, c2 = piv[1, 0], piv[1, 1], piv[1, 2]
    one = jnp.where(b1 == 0, 0, 1)
    two = 1 - one

    def keep(i, j):
        return pat[j, i].astype(F32)

    def dot(left, right):
        return jnp.dot(left, right, preferred_element_type=F32)

    own1 = keep(b1, col)
    cross12 = keep(b1, c2)
    lead[...] = (dot(corners[two], inv[0]) * keep(b2, c1)).astype(BF)

    @pl.when(col == c1)
    def _():
        upper[...] = lead[...]

    @pl.when(col != c1)
    def _():
        old = tops[two].astype(F32) * keep(b2, col)
        upper[...] = (old - dot(lead[...], tops[one]) * own1).astype(BF)

    for load in loads:
        load.wait()

    def slot(s, carry):
        here = s * nrow + row
        held = jnp.where(here == b1, a1, jnp.where(here == b2, a2, here))
        turned = s - jnp.where(row == nrow // 2, jnp.where(b1 == 0, a1, a2), jnp.where(b1 == 0, a2, a1)) // nrow
        turned = jnp.where(turned < 0, turned + slots, turned)
        give = jnp.logical_or(row == nrow // 2, row == nrow // 2 - 1)
        unit = jnp.where(give, turned, jnp.where(row < nrow // 2, s, slots - 1 - s))
        old = jnp.where(here == held, blocks[s], swapped[...]).astype(F32) * keep(held, col)
        left1 = (dot(panels[0, unit], inv[0]) * keep(held, c1)).astype(BF)
        step1 = (old - dot(left1, tops[one]) * own1).astype(BF)
        column2 = panels[1, unit].astype(F32) * keep(held, c2) - dot(left1, corners[one]) * cross12
        left2 = dot(column2.astype(BF), inv[1]).astype(BF)
        out[s] = (step1.astype(F32) - dot(left2, upper[...])).astype(BF)

        @pl.when(col == c1)
        def _():
            out[s] = left1

        @pl.when(col == c2)
        def _():
            out[s] = left2

        @pl.when(here == a1)
        def _():
            out[s] = (tops[one].astype(F32) * own1).astype(BF)

        @pl.when(here == a2)
        def _():
            out[s] = upper[...]

        return carry

    lax.fori_loop(0, slots, slot, 0)


def run_update(pivots, pattern, blocks, panels, corners, tops, swapped, inverses):
    slots, size, width = blocks.shape
    smem, vmem = pl.BlockSpec(memory_space=pltpu.SMEM), pl.BlockSpec(memory_space=pltpu.VMEM)
    far = pl.BlockSpec(memory_space=pl.ANY)
    return pl.pallas_call(
        update,
        out_shape=jax.ShapeDtypeStruct(blocks.shape, BF),
        in_specs=[smem, smem, far, far, vmem, vmem, far, vmem],
        out_specs=vmem,
        scratch_shapes=[pltpu.VMEM((size, width), BF)] * 2
        + [pltpu.VMEM(blocks.shape, BF), pltpu.VMEM(panels.shape, BF), pltpu.VMEM((size, width), BF)]
        + [pltpu.SemaphoreType.DMA((3,))],
        name="update",
    )(pivots, pattern, blocks, panels, corners, tops, swapped, inverses)


def local(matrix, pattern, inverses, pivots):
    slots, size, _, width = matrix.shape
    blocks = matrix.reshape(slots, size, width)
    moved = run_gather(pivots, blocks)
    return run_update(pivots, pattern.T, blocks, *moved, inverses).reshape(matrix.shape)


def solution(mesh):
    placed = (P(None, "prow", None, "pcol"), P(), P(), P())
    return jax.shard_map(
        local, mesh=mesh, in_specs=placed, out_specs=P(None, "prow", None, "pcol"), check_vma=False
    )
```
